128 devices in a mesh: zone: 4 (over y), block: 32 (over x, z, core).
Axes of the slice: x: 4, y: 4, z: 4, core: 2. Of those that a mesh axis runs over, the one named last changes fastest.
Arguments:
- start_state: float32 [5, 4, 4096, 512], P(None, 'zone', 'block'), may hold values from -6 to 6
- diffusivity: float32 [4, 4096, 512], P('zone', 'block'), may hold values from 0.02 to 0.2
- donor_map: int32 [4, 4, 4096], P(None, 'zone'), may hold values from 0 to 4095, as said below
- donor_weight: float32 [4, 4, 4096], P(None, 'zone'), may hold values from 0 to 1
- coupling: float32 [5, 5], replicated, may hold values from -0.15 to 0.15
- final_cotangent: float32 [5, 4, 4096, 512], P(None, 'zone', 'block'), may hold values from -6 to 6
- wall_area: float32 [4, 12288], P('zone', 'block'), may hold values from 0.5 to 2
- wall_projection: float32 [3, 5], replicated, may hold values from -2.5 to 2.5
- center_ids: int32 [4, 8, 12288], P('zone', None, 'block'), may hold values from 0 to 32767
- center_dist: float32 [4, 8, 12288], P('zone', None, 'block'), may hold values from 0 to 0.95
Outputs:
- adjoint_start: float32 [5, 4, 4096, 512], P(None, 'zone', 'block')
- shape_gradient: float32 [3, 32768], P(None, ('zone', 'block'))
The draws below stay inside these ranges and needn't reach their ends.
Inputs may be any that keep to these rules, and one draw needn't show every extreme that they name: For each step n and zone z there is an offset t, and donor_map[n, z, a] = (a + t + e) mod 4096 with e in 0 to 4.
All inputs are finite; a program needn't handle non-finite values.
Results may differ from the reference program's by a relative error of at most 0.0003.
Values sent between devices are 32-bit elements; how exact they have to be, the bound alone decides.
A program may use at most 128 MiB of HBM per device.

```python
import math
import jax
import jax.numpy as jnp
from jax import lax

NV = 5
STEPS = 4
KSUP = 8
NODES = 3
NRAD = 512
NZONE = 4
NA = 4096
WALL = 12288
CP = 32768


def draw_donor_map(key, part):
    first_key, second_key = jax.random.split(jax.random.fold_in(key, 11))
    offset = jax.random.randint(first_key, (STEPS, NZONE, 1), 0, NA)
    jitter = jax.random.randint(second_key, (STEPS, NZONE, NA), 0, 5)
    positions = jnp.arange(NA, dtype=jnp.int32)[None, None, :]
    return ((positions + offset + jitter) % NA).astype(jnp.int32)


def place_ends(result, own_key, low, largest):
    dims = result.shape
    spot = [jax.random.randint(jax.random.fold_in(own_key, axis), (), 0, dims[axis]) for axis in range(len(dims))]
    result = result.at[tuple(spot)].set(low)
    longest = dims.index(max(dims))
    spot[longest] = (spot[longest] + 1) % dims[longest]
    return result.at[tuple(spot)].set(largest)


def block_scale(rng, dims, cuts, least, largest):
    gain, own = 1.0, jax.random.fold_in(rng, 6)
    for dim, parts in cuts:
        steps = jnp.exp(jax.random.uniform(jax.random.fold_in(own, dim), (parts,), jnp.float32, least / len(cuts), largest / len(cuts)))
        gain = gain * jnp.repeat(steps, dims[dim] // parts).reshape([-1 if axis == dim else 1 for axis in range(len(dims))])
    return gain


def scatter_about(key, dims, scale, reach, pieces=(), kind=jnp.bfloat16):
    entries = jax.random.normal(key, dims, jnp.float32) * scale
    if len(pieces) > 0:
        entries = block_scale(key, dims, pieces, -0.22, 0.18) * entries
    return jnp.clip(entries, min=-reach, max=reach).astype(kind)


def setup_inputs(seed: int = 0) -> dict:
    splits = jax.random.split(jax.random.key(seed), 11)
    start_state = scatter_about(splits[0], (NV, NZONE, NA, NRAD), 1.0, 6.0, ((1, 4), (2, 32)), jnp.float32)
    diffusivity = jnp.clip(jnp.exp(math.log(0.2) - 2.3025851 * jax.random.uniform(splits[1], (NZONE, NA, NRAD), jnp.float32) ** block_scale(splits[1], (NZONE, NA, NRAD), ((0, 4), (1, 32)), -0.2, 0.2)), 0.02, 0.2)
    donor_map = draw_donor_map(jax.random.fold_in(splits[10], 71), 0)
    donor_weight = jnp.clip(1.0 * jax.random.uniform(splits[3], (STEPS, NZONE, NA), jnp.float32) ** block_scale(splits[3], (STEPS, NZONE, NA), ((1, 4),), -0.2, 0.2), 0.0, 1.0)
    coupling = jnp.clip(jax.random.uniform(splits[4], (NV, NV), jnp.float32, -0.15, 0.15), -0.15, 0.15)
    final_cotangent = scatter_about(splits[5], (NV, NZONE, NA, NRAD), 1.0, 6.0, ((1, 4), (2, 32)), jnp.float32)
    wall_area = jnp.clip(jnp.exp(math.log(2.0) - 1.3862944 * jax.random.uniform(splits[6], (NZONE, WALL), jnp.float32) ** block_scale(splits[6], (NZONE, WALL), ((0, 4), (1, 32)), -0.2, 0.2)), 0.5, 2.0)
    wall_projection = scatter_about(splits[7], (3, NV), NV ** -0.5, 2.5, (), jnp.float32)
    center_ids = place_ends(jax.random.randint(splits[8], (NZONE, KSUP, WALL), 0, CP), jax.random.fold_in(splits[8], 1), 0, CP - 1).astype(jnp.int32)
    center_dist = jnp.clip(0.95 * jax.random.uniform(splits[9], (NZONE, KSUP, WALL), jnp.float32) ** block_scale(splits[9], (NZONE, KSUP, WALL), ((0, 4), (2, 32)), -0.2, 0.2), 0.0, 0.95)
    return {"start_state": start_state, "diffusivity": diffusivity, "donor_map": donor_map, "donor_weight": donor_weight, "coupling": coupling, "final_cotangent": final_cotangent, "wall_area": wall_area, "wall_projection": wall_projection, "center_ids": center_ids, "center_dist": center_dist}


def advance(field, diffusivity, donor_rows, donor_share, coupling):
    row_total = field.shape[2]
    zone_total = field.shape[1]
    outer_face = field[:, :, :, -1]
    partner_face = outer_face[:, jnp.bitwise_xor(jnp.arange(zone_total, dtype=jnp.int32), 1)]
    second_rows = (donor_rows + 1) % row_total
    donor_first = jnp.take_along_axis(partner_face, donor_rows[None], axis=2)
    donor_second = jnp.take_along_axis(partner_face, second_rows[None], axis=2)
    ghost = donor_share[None] * donor_first + (1.0 - donor_share[None]) * donor_second
    outward = jnp.concatenate([field[..., 1:], ghost[..., None]], axis=-1)
    inward = jnp.concatenate([jnp.zeros_like(field[..., :1]), field[..., :-1]], axis=-1)
    laplace = jnp.roll(field, -1, axis=2) + jnp.roll(field, 1, axis=2) + outward + inward - 4.0 * field
    reaction = jnp.einsum('vw,wzar->vzar', coupling, jnp.tanh(field), precision=lax.Precision.HIGHEST)
    return field + diffusivity[None] * laplace - reaction

def reference(start_state, diffusivity, donor_map, donor_weight, coupling, final_cotangent, wall_area, wall_projection, center_ids, center_dist):
    history = [start_state]
    for time_step in range(STEPS - 1):
        history.append(advance(history[-1], diffusivity, donor_map[time_step], donor_weight[time_step], coupling))
    adjoint = final_cotangent
    wall_product = jnp.zeros(start_state.shape[:3], jnp.float32)
    for time_step in reversed(range(STEPS)):
        wall_product = wall_product + adjoint[..., 0] * history[time_step][..., 0]

        def forward(state, time_step=time_step):
            return advance(state, diffusivity, donor_map[time_step], donor_weight[time_step], coupling)
        _, pullback = jax.vjp(forward, history[time_step])
        adjoint = pullback(adjoint)[0]
    repeated = jnp.repeat(wall_product, NODES, axis=2)
    sensitivity = wall_area[None] * jnp.einsum('cv,vzw->czw', wall_projection, repeated, precision=lax.Precision.HIGHEST)
    kernel = (1.0 - center_dist) ** 4 * (4.0 * center_dist + 1.0)
    weighted = kernel[None] * sensitivity[:, :, None, :]
    gradient = jnp.zeros((3, CP), jnp.float32).at[:, center_ids.reshape(-1)].add(weighted.reshape(3, -1))
    return (adjoint, gradient)
```

```python
import functools

import jax
import jax.numpy as jnp
from jax import lax
from jax.experimental import pallas as pl
from jax.experimental.pallas import tpu as pltpu
from jax.sharding import PartitionSpec as P

MESH = pl.DeviceIdType.MESH
F32 = jnp.float32
V = 5
KU = 6
KL = 4
OFF_L = V * KU
OFF_K = OFF_L + V * KL
OFF_M = OFF_K + KU
OFF_W = OFF_M + 4
CHUNK = 64
ROWS = 160


def lane_of(shape):
    return lax.broadcasted_iota(jnp.int32, shape, len(shape) - 1)


def place():
    y = lax.axis_index("zone")
    b = lax.axis_index("block")
    return y, b, b // 8, (b // 2) % 4, b % 2


def block_of(x, z, c):
    return x * 8 + z * 2 + c


def remote(src, dst, send, recv, y, b):
    return pltpu.make_async_remote_copy(
        src_ref=src, dst_ref=dst, send_sem=send, recv_sem=recv, device_id=(y, b), device_id_type=MESH
    )


def exchange_kernel(
    u_hbm, k_hbm, l_hbm, m_hbm, w_hbm, gat, hu, hl, hk,
    chunk, ut, lt, kt, mt, wt, local_sem, halo_s, halo_r, first_s, first_r, ph_s, ph_r, core_s, core_r,
):
    y, b, x, z, c = place()
    q = y % 2
    yp = y + 1 - 2 * q
    b0 = b - c
    nxt, prv = (b + 1) % 32, (b + 31) % 32

    loads = [
        pltpu.make_async_copy(u_hbm.at[:, 0, :, pl.ds(384, 128)], ut, local_sem.at[0]),
        pltpu.make_async_copy(l_hbm.at[:, 0, :, pl.ds(384, 128)], lt, local_sem.at[1]),
        pltpu.make_async_copy(k_hbm.at[0, :, pl.ds(384, 128)], kt, local_sem.at[2]),
        pltpu.make_async_copy(m_hbm.at[:, 0, pl.ds(pl.multiple_of(b * 128, 128), 128)], mt, local_sem.at[3]),
        pltpu.make_async_copy(w_hbm.at[:, 0, pl.ds(pl.multiple_of(b * 128, 128), 128)], wt, local_sem.at[4]),
    ]
    for copy in loads:
        copy.start()

    barrier = pltpu.get_barrier_semaphore()
    peers = [(y, nxt), (y, prv), (yp, b0), (yp, b0 + 1), (y, b0 + 1 - c)]
    for d in (1, 2, 3):
        peers.append((y, block_of((x + d) % 4, z, c)))
        peers.append((y, block_of(x, (z + d) % 4, c)))
    for peer in peers:
        pl.semaphore_signal(barrier, inc=1, device_id=peer, device_id_type=MESH)
    pl.semaphore_wait(barrier, len(peers))

    halo = []
    for n, (src, dst) in enumerate(((u_hbm, hu), (l_hbm, hl), (k_hbm, hk))):
        def rows(r):
            return src.at[:, 0, pl.ds(r, 8), :] if len(src.shape) == 4 else src.at[0, pl.ds(r, 8), :]
        halo.append(remote(rows(120), dst.at[0], halo_s.at[n], halo_r.at[n], y, nxt))
        halo.append(remote(rows(0), dst.at[1], halo_s.at[3 + n], halo_r.at[3 + n], y, prv))
    for copy in halo:
        copy.start()

    for copy in loads:
        copy.wait()
    for v in range(V):
        chunk[KU * v : KU * (v + 1), :] = ut[v].T[128 - KU :, :]
        chunk[OFF_L + KL * v : OFF_L + KL * (v + 1), :] = lt[v].T[128 - KL :, :]
    chunk[OFF_K : OFF_K + KU, :] = kt[...].T[128 - KU :, :]
    chunk[OFF_M : OFF_M + 4, :] = mt[...].astype(F32)
    chunk[OFF_W : OFF_W + 4, :] = wt[...]

    def slot(zone, xx, j):
        return gat.at[zone, xx, j]

    here = slot(q, x, z * 2 + c)
    across = remote(chunk, here, first_s.at[0], first_r.at[c], yp, b0 + q)
    across.start()
    beside = remote(chunk, here, first_s.at[1], first_r.at[2], y, b0 + q)

    @pl.when(c == q)
    def _():
        gat[q, x, z * 2 + c] = chunk[...]
        remote(chunk, slot(q, x, z * 2 + 1 - c), first_s.at[1], first_r.at[2], y, b0 + q).wait_recv()

    @pl.when(c != q)
    def _():
        beside.start()
        for j in range(2):
            remote(chunk, slot(1 - q, x, z * 2 + j), first_s.at[0], first_r.at[j], yp, b0 + q).wait_recv()
        beside.wait_send()

    across.wait_send()

    def along(part_first, part_second, first_is_x):
        for stage in range(2):
            use_x = first_is_x == (stage == 0)
            copies = []
            for d in (1, 2, 3):
                to = block_of((x + d) % 4, z, c) if use_x else block_of(x, (z + d) % 4, c)
                src = (part_first if stage == 0 else part_second)(x, z)
                copies.append(remote(src, src, ph_s.at[3 * stage + d - 1], ph_r.at[3 * stage + d - 1], y, to))
            for copy in copies:
                copy.start()
            for copy in copies:
                copy.wait()

    @pl.when(c == 0)
    def _():
        along(lambda xx, zz: gat.at[0, xx, pl.ds(zz * 2, 2)], lambda xx, zz: gat.at[0, :, pl.ds(zz * 2, 2)], True)

    @pl.when(c == 1)
    def _():
        along(lambda xx, zz: gat.at[1, xx, pl.ds(zz * 2, 2)], lambda xx, zz: gat.at[1, xx], False)

    swap = remote(gat.at[c], gat.at[c], core_s, core_r, y, b0 + 1 - c)
    swap.start()
    swap.wait()
    for copy in halo:
        copy.wait()


def exchange(u, kappa, lam, dmap, dweight):
    any_ = pl.BlockSpec(memory_space=pl.ANY)
    vmem = pl.BlockSpec(memory_space=pltpu.VMEM)
    dma = pltpu.SemaphoreType.DMA
    return pl.pallas_call(
        exchange_kernel,
        out_shape=(
            jax.ShapeDtypeStruct((2, 4, 8, CHUNK, 128), F32),
            jax.ShapeDtypeStruct((2, V, 8, 512), F32),
            jax.ShapeDtypeStruct((2, V, 8, 512), F32),
            jax.ShapeDtypeStruct((2, 8, 512), F32),
        ),
        in_specs=[any_] * 5,
        out_specs=(vmem,) * 4,
        scratch_shapes=[
            pltpu.VMEM((CHUNK, 128), F32),
            pltpu.VMEM((V, 128, 128), F32),
            pltpu.VMEM((V, 128, 128), F32),
            pltpu.VMEM((128, 128), F32),
            pltpu.VMEM((4, 128), jnp.int32),
            pltpu.VMEM((4, 128), F32),
            dma((5,)), dma((6,)), dma((6,)), dma((2,)), dma((3,)), dma((6,)), dma((6,)), dma, dma,
        ],
        compiler_params=pltpu.CompilerParams(collective_id=0, has_side_effects=True),
        name="exchange",
    )(u, kappa, lam, dmap, dweight)


def fill_tiles(dst, src_vmem, halo, variables):
    pass


def main_forward(n, us, ds, kap, coup, tiles, ghost):
    lane = lane_of((8, 128))
    cf = [[coup[v, w] for w in range(V)] for v in range(V)]
    src, dst, dd = us[n], us[n + 1], ds[n]

    def body(i, carry):
        r = pl.multiple_of(8 + i * 8, 8)
        rows = pl.ds(r, 8)
        for t in tiles:
            k = kap[t, rows, :]
            cur = [src[v, t, rows, :] for v in range(V)]
            th = [jnp.tanh(a) for a in cur]
            for v in range(V):
                if t == 0:
                    left = jnp.where(lane == 127, 0.0, cur[v])
                else:
                    left = jnp.where(lane == 127, src[v, t - 1, rows, :], cur[v])
                if t < 3:
                    right = jnp.where(lane == 0, src[v, t + 1, rows, :], cur[v])
                elif ghost is None:
                    right = jnp.where(lane == 0, 0.0, cur[v])
                else:
                    g = pltpu.roll(ghost[rows, :], (128 - (n * V + v)) % 128, 1)
                    right = jnp.where(lane == 0, g, cur[v])
                lap = (
                    src[v, t, pl.ds(r - 1, 8), :] + src[v, t, pl.ds(r + 1, 8), :]
                    + pltpu.roll(left, 1, 1) + pltpu.roll(right, 127, 1) - 4.0 * cur[v]
                )
                react = cf[v][0] * th[0]
                for w in range(1, V):
                    react = react + cf[v][w] * th[w]
                dst[v, t, rows, :] = cur[v] + k * lap - react
                dd[v, t, rows, :] = 1.0 - th[v] * th[v]
        return carry

    lax.fori_loop(0, 18, body, 0)


def main_adjoint(n, us, ds, ls, ss, kap, coup, tiles, back, hsum, out):
    lane = lane_of((8, 128))
    cf = [[coup[w, v] for w in range(V)] for v in range(V)]
    m = 3 - n
    lam, sca = ls[m], ss[m]

    def body(i, carry):
        r = pl.multiple_of(8 + i * 8, 8)
        rows = pl.ds(r, 8)
        for t in tiles:
            cur = [lam[v, t, rows, :] for v in range(V)]
            for v in range(V):
                s = sca[v, t, rows, :]
                if t == 0:
                    left = jnp.where(lane == 127, 0.0, s)
                else:
                    left = jnp.where(lane == 127, sca[v, t - 1, rows, :], s)
                right = jnp.where(lane == 0, sca[v, t + 1, rows, :] if t < 3 else 0.0, s)
                lap = (
                    sca[v, t, pl.ds(r - 1, 8), :] + sca[v, t, pl.ds(r + 1, 8), :]
                    + pltpu.roll(left, 1, 1) + pltpu.roll(right, 127, 1) - 4.0 * s
                )
                if n == 3:
                    th = jnp.tanh(us[3][v, t, rows, :])
                    d = 1.0 - th * th
                else:
                    d = ds[n][v, t, rows, :]
                pulled = cf[v][0] * cur[0]
                for w in range(1, V):
                    pulled = pulled + cf[v][w] * cur[w]
                new = cur[v] + lap - d * pulled
                if t == 3 and back is not None:
                    f = pltpu.roll(back[rows, :], 127 - (15 + n * V + v), 1)
                    new = new + jnp.where(lane == 127, f, 0.0)
                if n > 0:
                    ls[m + 1][v, t, rows, :] = new
                    ss[m + 1][v, t, rows, :] = kap[t, rows, :] * new
                else:
                    out[v, t, pl.ds(pl.multiple_of(r - 16, 8), 8), :] = new
                if t == 0 and hsum is not None:
                    p = cur[v] * us[n][v, t, rows, :]
                    if n == 3:
                        hsum[v, rows, :] = p
                    else:
                        hsum[v, rows, :] = hsum[v, rows, :] + p
        return carry

    if n > 0:
        lax.fori_loop(0, 18, body, 0)
    else:
        lax.fori_loop(1, 17, body, 0)


def rows_beside(a):
    lane = lane_of(a.shape)
    up = pltpu.roll(jnp.where(lane == 127, pltpu.roll(a, 1, 0), a), 1, 1)
    down = pltpu.roll(jnp.where(lane == 0, pltpu.roll(a, 31, 0), a), 127, 1)
    return up + down


def put_ring(ring, a):
    ring[0:32, :] = a
    ring[32:64, :] = a
    ring[64:72, :] = a[0:8]


def shifted(ring, amount):
    lane = lane_of((32, 128))
    high, low = amount // 128, amount % 128
    first = ring[pl.ds(high, 32), :]
    second = ring[pl.ds(high + 1, 32), :]
    return pltpu.roll(jnp.where(lane < low, second, first), (128 - low) % 128, 1)


def strips(gat, q, coup, su, sd, sl, sk, tap, shift, ring, tring, face):
    row = lax.broadcasted_iota(jnp.int32, (32, 128), 0) * 128 + lane_of((32, 128))

    def get(zone, j):
        return gat[zone, pl.ds(j, 32, stride=CHUNK), :]

    def unpack(zone, carry):
        for v in range(V):
            for k in range(KU):
                su[0, zone, v, k] = get(zone, v * KU + KU - 1 - k)
            for k in range(KL):
                sl[0, zone, v, k] = get(zone, OFF_L + v * KL + KL - 1 - k)
        for k in range(KU):
            sk[zone, k] = get(zone, OFF_K + KU - 1 - k)
        for n in range(4):
            d = get(zone, OFF_M + n).astype(jnp.int32) - row
            base = d[0:1, 0:1]
            d = d - base
            d = jnp.where(d > 2048, d - 4096, d)
            d = jnp.where(d > 2048, d - 4096, d)
            d = jnp.where(d < -2048, d + 4096, d)
            d = jnp.where(d < -2048, d + 4096, d)
            least = jnp.min(d)
            e = d - least
            w = get(zone, OFF_W + n)
            shift[zone, n] = (base[0, 0] + least + 8192) % 4096
            for j in range(6):
                tap[zone, n, j] = jnp.where(e == j, w, 0.0) + jnp.where(e == j - 1, 1.0 - w, 0.0)
        return carry

    lax.fori_loop(0, 2, unpack, 0)

    for n in range(3):
        def faces(zone, carry):
            for v in range(V):
                put_ring(ring.at[zone, v], su[n, zone, v, 0])
            return carry

        lax.fori_loop(0, 2, faces, 0)

        def step(zone, carry):
            ghost = [jnp.zeros((32, 128), F32)] * V
            t = shift[zone, n]
            for j in range(6):
                cj = tap[zone, n, j]
                for v in range(V):
                    ghost[v] = ghost[v] + cj * shifted(ring.at[1 - zone, v], (t + j) % 4096)
            for v in range(V):
                face[zone, n * V + v] = ghost[v]
            for k in range(KU - 1 - n):
                cur = [su[n, zone, v, k] for v in range(V)]
                th = [jnp.tanh(a) for a in cur]
                kk = sk[zone, k]
                for v in range(V):
                    outward = ghost[v] if k == 0 else su[n, zone, v, k - 1]
                    lap = rows_beside(cur[v]) + outward + su[n, zone, v, k + 1] - 4.0 * cur[v]
                    react = coup[v, 0] * th[0]
                    for w in range(1, V):
                        react = react + coup[v, w] * th[w]
                    su[n + 1, zone, v, k] = cur[v] + kk * lap - react
                    if k < n:
                        sd[n, zone, v, k] = 1.0 - th[v] * th[v]
            return carry

        lax.fori_loop(0, 2, step, 0)

    for n in (3, 2, 1, 0):
        m = 3 - n

        def taps(zone, carry):
            for v in range(V):
                put_ring(ring.at[zone, v], sk[zone, 0] * sl[m, zone, v, 0])
            return carry

        lax.fori_loop(0, 2, taps, 0)

        def back(zone, carry):
            other = 1 - zone
            acc = [jnp.zeros((32, 128), F32)] * V
            t = shift[other, n]
            for j in range(6):
                put_ring(tring, tap[other, n, j])
                amount = (8192 - t - j) % 4096
                cj = shifted(tring, amount)
                for v in range(V):
                    acc[v] = acc[v] + cj * shifted(ring.at[other, v], amount)
            for v in range(V):
                face[zone, 15 + n * V + v] = acc[v]
            for k in range(n):
                cur = [sl[m, zone, v, k] for v in range(V)]
                kk = sk[zone, k]
                for v in range(V):
                    s = kk * cur[v]
                    lap = rows_beside(s) + sk[zone, k + 1] * sl[m, zone, v, k + 1] - 4.0 * s
                    if k == 0:
                        lap = lap + acc[v]
                    else:
                        lap = lap + sk[zone, k - 1] * sl[m, zone, v, k - 1]
                    if n == 3:
                        th = jnp.tanh(su[3, zone, v, k])
                        d = 1.0 - th * th
                    else:
                        d = sd[n, zone, v, k]
                    pulled = coup[0, v] * cur[0]
                    for w in range(1, V):
                        pulled = pulled + coup[w, v] * cur[w]
                    sl[m + 1, zone, v, k] = cur[v] + lap - d * pulled
            return carry

        if n > 0:
            lax.fori_loop(0, 2, back, 0)
        else:
            back(q, 0)


def face_columns(face, q, b, cols):
    pad = jnp.zeros((128 - 35, 128), F32)
    for part, dst, size, lo in (((b + 31) % 32, 8, 8, 120), (b, 16, 128, 0), ((b + 1) % 32, 144, 8, 0)):
        rows = face[q, pl.ds(part, 35, stride=32), :]
        cols[dst : dst + size, :] = jnp.concatenate([rows, pad], axis=0).T[lo : lo + size, :]


def scatter_points(hsum, area, proj, ids, dist, partial):
    lane = lane_of((128, 128))
    hs = [hsum[v, 16:144, :] for v in range(V)]
    acc = jnp.zeros((128, 128), F32)
    for c in range(3):
        col = proj[c, 0] * hs[0]
        for v in range(1, V):
            col = col + proj[c, v] * hs[v]
        acc = acc + jnp.where(lane == c, pltpu.roll(col, c, 1), 0.0)
    spread = (
        lax.broadcasted_iota(jnp.int32, (128, 384), 1) // 3 == lax.broadcasted_iota(jnp.int32, (128, 384), 0)
    ).astype(F32)
    sens = lax.dot_general(
        acc, spread, (((0,), (0,)), ((), ())), precision=lax.Precision.HIGHEST, preferred_element_type=F32
    )
    sens = [sens[c : c + 1, :] * area[...] for c in range(3)]
    sub_a = lax.broadcasted_iota(jnp.int32, (128, 128), 0)
    sub_b = lax.broadcasted_iota(jnp.int32, (256, 128), 0)
    total = jnp.zeros((384, 256), F32)
    for k in range(8):
        dk = dist[k : k + 1, :]
        om = 1.0 - dk
        om = om * om
        phi = om * om * (4.0 * dk + 1.0)
        idk = ids[k : k + 1, :]
        for wt in range(3):
            cut = slice(wt * 128, (wt + 1) * 128)
            idt = idk[:, cut]
            ch = idt // 256
            rowid = (ch % 2) * 64 + ((ch // 8) % 4) * 16 + ((ch // 2) % 4) * 4 + ch // 32
            mask = sub_a == rowid
            high, low = [], []
            for c in range(3):
                val = phi[:, cut] * sens[c][:, cut]
                hi = val.astype(jnp.bfloat16).astype(F32)
                high.append(jnp.where(mask, hi, 0.0).astype(jnp.bfloat16))
                low.append(jnp.where(mask, val - hi, 0.0).astype(jnp.bfloat16))
            left = jnp.concatenate([jnp.concatenate(high, axis=0), jnp.concatenate(low, axis=0)], axis=1)
            onehot = jnp.where(sub_b == idt % 256, 1.0, 0.0).astype(jnp.bfloat16)
            right = jnp.concatenate([onehot, onehot], axis=1)
            total = total + lax.dot_general(
                left, right, (((1,), (1,)), ((), ())), preferred_element_type=F32
            )
    for c in range(3):
        partial[c] = total[c * 128 : (c + 1) * 128, :]


def local_kernel(
    coup, proj, u_hbm, k_hbm, l_hbm, gat, hu, hl, hk, area, ids, dist, out_hbm, partial,
    u0, u1, u2, u3, d0, d1, d2, l4, l3, l2, l1, s4, s3, s2, s1, kap, hsum, outv,
    su, sd, sl, sk, tap, ring, tring, face, cols, shift, sem, osem,
):
    y, b, x, z, c = place()
    q = y % 2
    us, ds, ls, ss = (u0, u1, u2, u3), (d0, d1, d2), (l4, l3, l2, l1), (s4, s3, s2, s1)
    loads = []
    for t in range(4):
        cut = pl.ds(t * 128, 128)
        own = pl.ds(16, 128)
        loads.append(pltpu.make_async_copy(u_hbm.at[:, 0, :, cut], u0.at[:, t, own, :], sem.at[3 * t]))
        loads.append(pltpu.make_async_copy(l_hbm.at[:, 0, :, cut], l4.at[:, t, own, :], sem.at[3 * t + 1]))
        loads.append(pltpu.make_async_copy(k_hbm.at[0, :, cut], kap.at[t, own, :], sem.at[3 * t + 2]))
    for copy in loads:
        copy.start()
    for t in range(4):
        cut = slice(t * 128, (t + 1) * 128)
        for side, r in ((0, 8), (1, 144)):
            kap[t, r : r + 8, :] = hk[side, :, cut]
            for v in range(V):
                u0[v, t, r : r + 8, :] = hu[side, v, :, cut]
                l4[v, t, r : r + 8, :] = hl[side, v, :, cut]
    for copy in loads:
        copy.wait()

    def scale(i, carry):
        rows = pl.ds(pl.multiple_of(8 + i * 8, 8), 8)
        for t in range(4):
            for v in range(V):
                s4[v, t, rows, :] = kap[t, rows, :] * l4[v, t, rows, :]
        return carry

    lax.fori_loop(0, 18, scale, 0)
    every = (0, 1, 2, 3)
    for n in range(3):
        main_forward(n, us, ds, kap, coup, every, None)
    for n in (3, 2, 1, 0):
        main_adjoint(n, us, ds, ls, ss, kap, coup, every, None, hsum, outv)
    scatter_points(hsum, area, proj, ids, dist, partial)
    strips(gat, q, coup, su, sd, sl, sk, tap, shift, ring, tring, face)
    face_columns(face.reshape(2, 35 * 32, 128), q, b, cols)
    for n in range(3):
        main_forward(n, us, ds, kap, coup, (3,), cols)
    for n in (3, 2, 1, 0):
        main_adjoint(n, us, ds, ls, ss, kap, coup, (3,), cols, None, outv)
    stores = []
    for t in range(4):
        stores.append(
            pltpu.make_async_copy(outv.at[:, t], out_hbm.at[:, 0, :, pl.ds(t * 128, 128)], osem.at[t])
        )
    for copy in stores:
        copy.start()
    for copy in stores:
        copy.wait()


def local_part(coup, proj, u, kappa, lam, gat, hu, hl, hk, area, ids, dist):
    any_ = pl.BlockSpec(memory_space=pl.ANY)
    vmem = pl.BlockSpec(memory_space=pltpu.VMEM)
    smem = pl.BlockSpec(memory_space=pltpu.SMEM)
    dma = pltpu.SemaphoreType.DMA
    cells = pltpu.VMEM((V, 4, ROWS, 128), F32)
    return pl.pallas_call(
        local_kernel,
        out_shape=(
            jax.ShapeDtypeStruct((V, 1, 128, 512), F32),
            jax.ShapeDtypeStruct((3, 128, 256), F32),
        ),
        in_specs=[smem, smem, any_, any_, any_, vmem, vmem, vmem, vmem, vmem, vmem, vmem],
        out_specs=(any_, vmem),
        scratch_shapes=[cells] * 15
        + [
            pltpu.VMEM((4, ROWS, 128), F32),
            pltpu.VMEM((V, ROWS, 128), F32),
            pltpu.VMEM((V, 4, 128, 128), F32),
            pltpu.VMEM((4, 2, V, KU, 32, 128), F32),
            pltpu.VMEM((3, 2, V, 2, 32, 128), F32),
            pltpu.VMEM((4, 2, V, KL, 32, 128), F32),
            pltpu.VMEM((2, KU, 32, 128), F32),
            pltpu.VMEM((2, 4, 6, 32, 128), F32),
            pltpu.VMEM((2, V, 72, 128), F32),
            pltpu.VMEM((72, 128), F32),
            pltpu.VMEM((2, 35, 32, 128), F32),
            pltpu.VMEM((ROWS, 128), F32),
            pltpu.SMEM((2, 4), jnp.int32),
            dma((12,)), dma((4,)),
        ],
        compiler_params=pltpu.CompilerParams(vmem_limit_bytes=62 * 1024 * 1024),
        name="cells",
    )(coup, proj, u, kappa, lam, gat.reshape(2, 32 * CHUNK, 128), hu, hl, hk, area, ids, dist)


def reduce_kernel(part, out, r1, q1, r2, q2, r3, q3, r4, ss, rs):
    y, b, x, z, c = place()
    barrier = pltpu.get_barrier_semaphore()
    peers = [(y, block_of(x, z, 1 - c))]
    for d in (1, 2, 3):
        peers.append((y, block_of((x + d) % 4, z, c)))
        peers.append((y, block_of(x, (z + d) % 4, c)))
        peers.append(((y + d) % 4, b))
    for peer in peers:
        pl.semaphore_signal(barrier, inc=1, device_id=peer, device_id_type=MESH)
    pl.semaphore_wait(barrier, len(peers))

    copy = remote(
        part.at[:, pl.ds(pl.multiple_of((1 - c) * 64, 64), 64), :], r1, ss.at[0], rs.at[0], y, block_of(x, z, 1 - c)
    )
    copy.start()
    copy.wait()
    own = pl.multiple_of(c * 64, 64)
    for j in range(4):
        q1[j] = part[:, pl.ds(own + j * 16, 16), :] + r1[:, j * 16 : (j + 1) * 16, :]

    copies = []
    for d in (1, 2, 3):
        to = (x + d) % 4
        copies.append(remote(q1.at[to], r2.at[d - 1], ss.at[d], rs.at[d], y, block_of(to, z, c)))
    for copy in copies:
        copy.start()
    for copy in copies:
        copy.wait()
    total = q1[x] + r2[0] + r2[1] + r2[2]
    for j in range(4):
        q2[j] = total[:, j * 4 : (j + 1) * 4, :]

    copies = []
    for d in (1, 2, 3):
        to = (z + d) % 4
        copies.append(remote(q2.at[to], r3.at[d - 1], ss.at[3 + d], rs.at[3 + d], y, block_of(x, to, c)))
    for copy in copies:
        copy.start()
    for copy in copies:
        copy.wait()
    total = q2[z] + r3[0] + r3[1] + r3[2]
    for j in range(4):
        q3[j] = total[:, j, :]

    copies = []
    for d in (1, 2, 3):
        to = (y + d) % 4
        copies.append(remote(q3.at[to], r4.at[d - 1], ss.at[6 + d], rs.at[6 + d], to, b))
    for copy in copies:
        copy.start()
    for copy in copies:
        copy.wait()
    out[...] = q3[y] + r4[0] + r4[1] + r4[2]


def reduce_points(partial):
    vmem = pl.BlockSpec(memory_space=pltpu.VMEM)
    dma = pltpu.SemaphoreType.DMA
    return pl.pallas_call(
        reduce_kernel,
        out_shape=jax.ShapeDtypeStruct((3, 256), F32),
        in_specs=[vmem],
        out_specs=vmem,
        scratch_shapes=[
            pltpu.VMEM((3, 64, 256), F32),
            pltpu.VMEM((4, 3, 16, 256), F32),
            pltpu.VMEM((3, 3, 16, 256), F32),
            pltpu.VMEM((4, 3, 4, 256), F32),
            pltpu.VMEM((3, 3, 4, 256), F32),
            pltpu.VMEM((4, 3, 256), F32),
            pltpu.VMEM((3, 3, 256), F32),
            dma((10,)), dma((10,)),
        ],
        compiler_params=pltpu.CompilerParams(collective_id=1, has_side_effects=True),
        name="reduce",
    )(partial)


def local(
    start_state, diffusivity, donor_map, donor_weight, coupling, final_cotangent,
    wall_area, wall_projection, center_ids, center_dist,
):
    gat, hu, hl, hk = exchange(start_state, diffusivity, final_cotangent, donor_map, donor_weight)
    adjoint, partial = local_part(
        coupling, wall_projection, start_state, diffusivity, final_cotangent, gat, hu, hl, hk,
        wall_area, center_ids[0], center_dist[0],
    )
    return adjoint, reduce_points(partial)


def solution(mesh):
    return jax.shard_map(
        local,
        mesh=mesh,
        in_specs=(
            P(None, "zone", "block", None),
            P("zone", "block", None),
            P(None, "zone", None),
            P(None, "zone", None),
            P(),
            P(None, "zone", "block", None),
            P("zone", "block"),
            P(),
            P("zone", None, "block"),
            P("zone", None, "block"),
        ),
        out_specs=(P(None, "zone", "block", None), P(None, ("zone", "block"))),
        check_vma=False,
    )
```

```python
import functools

import jax
import jax.numpy as jnp
from jax import lax
from jax.experimental import pallas as pl
from jax.experimental.pallas import tpu as pltpu
from jax.sharding import PartitionSpec as P

MESH = pl.DeviceIdType.MESH
F32 = jnp.float32
V = 5
KU = 6
KL = 4
OFF_L = V * KU
OFF_K = OFF_L + V * KL
OFF_M = OFF_K + KU
OFF_W = OFF_M + 4
CHUNK = 64
ROWS = 160


def lane_of(shape):
    return lax.broadcasted_iota(jnp.int32, shape, len(shape) - 1)


def place():
    y = lax.axis_index("zone")
    b = lax.axis_index("block")
    return y, b, b // 8, (b // 2) % 4, b % 2


def block_of(x, z, c):
    return x * 8 + z * 2 + c


def remote(src, dst, send, recv, y, b):
    return pltpu.make_async_remote_copy(
        src_ref=src, dst_ref=dst, send_sem=send, recv_sem=recv, device_id=(y, b), device_id_type=MESH
    )


def over_rows(body, first, count, unroll):
    def several(i, carry):
        for j in range(unroll):
            body(first + i * unroll + j)
        return carry

    lax.fori_loop(0, count // unroll, several, 0)


def main_forward(n, us, ds, kap, coup, tiles, ghost):
    lane = lane_of((8, 128))
    cf = [[coup[v, w] for w in range(V)] for v in range(V)]
    src, dst, dd = us[n], us[n + 1], ds[n]

    def body(i):
        r = pl.multiple_of(8 + i * 8, 8)
        rows = pl.ds(r, 8)
        for t in tiles:
            k = kap[t, rows, :]
            cur = [src[v, t, rows, :] for v in range(V)]
            th = [jnp.tanh(a) for a in cur]
            for v in range(V):
                if t == 0:
                    left = jnp.where(lane == 127, 0.0, cur[v])
                else:
                    left = jnp.where(lane == 127, src[v, t - 1, rows, :], cur[v])
                if t < 3:
                    right = jnp.where(lane == 0, src[v, t + 1, rows, :], cur[v])
                elif ghost is None:
                    right = jnp.where(lane == 0, 0.0, cur[v])
                else:
                    g = pltpu.roll(ghost[rows, :], (128 - (n * V + v)) % 128, 1)
                    right = jnp.where(lane == 0, g, cur[v])
                lap = (
                    src[v, t, pl.ds(r - 1, 8), :] + src[v, t, pl.ds(r + 1, 8), :]
                    + pltpu.roll(left, 1, 1) + pltpu.roll(right, 127, 1) - 4.0 * cur[v]
                )
                react = cf[v][0] * th[0]
                for w in range(1, V):
                    react = react + cf[v][w] * th[w]
                dst[v, t, rows, :] = cur[v] + k * lap - react
                dd[v, t, rows, :] = 1.0 - th[v] * th[v]

    over_rows(body, 0, 18, 6 if len(tiles) == 1 else 2)


def main_adjoint(n, us, ds, ls, ss, kap, coup, tiles, back, hsum, out):
    lane = lane_of((8, 128))
    cf = [[coup[w, v] for w in range(V)] for v in range(V)]
    m = 3 - n
    lam, sca = ls[m], ss[m]

    def body(i):
        r = pl.multiple_of(8 + i * 8, 8)
        rows = pl.ds(r, 8)
        for t in tiles:
            cur = [lam[v, t, rows, :] for v in range(V)]
            for v in range(V):
                s = sca[v, t, rows, :]
                if t == 0:
                    left = jnp.where(lane == 127, 0.0, s)
                else:
                    left = jnp.where(lane == 127, sca[v, t - 1, rows, :], s)
                right = jnp.where(lane == 0, sca[v, t + 1, rows, :] if t < 3 else 0.0, s)
                lap = (
                    sca[v, t, pl.ds(r - 1, 8), :] + sca[v, t, pl.ds(r + 1, 8), :]
                    + pltpu.roll(left, 1, 1) + pltpu.roll(right, 127, 1) - 4.0 * s
                )
                if n == 3:
                    th = jnp.tanh(us[3][v, t, rows, :])
                    d = 1.0 - th * th
                else:
                    d = ds[n][v, t, rows, :]
                pulled = cf[v][0] * cur[0]
                for w in range(1, V):
                    pulled = pulled + cf[v][w] * cur[w]
                new = cur[v] + lap - d * pulled
                if t == 3 and back is not None:
                    f = pltpu.roll(back[rows, :], 127 - (15 + n * V + v), 1)
                    new = new + jnp.where(lane == 127, f, 0.0)
                if n > 0:
                    ls[m + 1][v, t, rows, :] = new
                    ss[m + 1][v, t, rows, :] = kap[t, rows, :] * new
                else:
                    out[v, t, pl.ds(pl.multiple_of(r - 16, 8), 8), :] = new
                if t == 0 and hsum is not None:
                    p = cur[v] * us[n][v, t, rows, :]
                    if n == 3:
                        hsum[v, rows, :] = p
                    else:
                        hsum[v, rows, :] = hsum[v, rows, :] + p

    if n > 0:
        over_rows(body, 0, 18, 6 if len(tiles) == 1 else 2)
    else:
        over_rows(body, 1, 16, 4 if len(tiles) == 1 else 2)


def rows_beside(a):
    lane = lane_of(a.shape)
    up = pltpu.roll(jnp.where(lane == 127, pltpu.roll(a, 1, 0), a), 1, 1)
    down = pltpu.roll(jnp.where(lane == 0, pltpu.roll(a, 31, 0), a), 127, 1)
    return up + down


def put_ring(ring, a):
    ring[0:32, :] = a
    ring[32:64, :] = a
    ring[64:72, :] = a[0:8]


def shifted(ring, amount):
    lane = lane_of((32, 128))
    high, low = amount // 128, amount % 128
    first = ring[pl.ds(high, 32), :]
    second = ring[pl.ds(high + 1, 32), :]
    return pltpu.roll(jnp.where(lane < low, second, first), (128 - low) % 128, 1)


def strips(gat, q, coup, su, sd, sl, sk, tap, shift, ring, tring, face, between):
    row = lax.broadcasted_iota(jnp.int32, (32, 128), 0) * 128 + lane_of((32, 128))

    def get(zone, j):
        return gat[zone, pl.ds(j, 32, stride=CHUNK), :]

    def unpack(zone, carry):
        for v in range(V):
            for k in range(KU):
                su[0, zone, v, k] = get(zone, v * KU + KU - 1 - k)
            for k in range(KL):
                sl[0, zone, v, k] = get(zone, OFF_L + v * KL + KL - 1 - k)
        for k in range(KU):
            sk[zone, k] = get(zone, OFF_K + KU - 1 - k)
        for n in range(4):
            d = get(zone, OFF_M + n).astype(jnp.int32) - row
            base = d[0:1, 0:1]
            d = d - base
            d = jnp.where(d > 2048, d - 4096, d)
            d = jnp.where(d > 2048, d - 4096, d)
            d = jnp.where(d < -2048, d + 4096, d)
            d = jnp.where(d < -2048, d + 4096, d)
            least = jnp.min(d)
            e = d - least
            w = get(zone, OFF_W + n)
            shift[zone, n] = (base[0, 0] + least + 8192) % 4096
            for j in range(6):
                tap[zone, n, j] = jnp.where(e == j, w, 0.0) + jnp.where(e == j - 1, 1.0 - w, 0.0)
        return carry

    lax.fori_loop(0, 2, unpack, 0)

    for n in range(3):
        def faces(zone, carry):
            for v in range(V):
                put_ring(ring.at[zone, v], su[n, zone, v, 0])
            return carry

        lax.fori_loop(0, 2, faces, 0)

        def step(zone, carry):
            ghost = [jnp.zeros((32, 128), F32)] * V
            t = shift[zone, n]
            for j in range(6):
                cj = tap[zone, n, j]
                for v in range(V):
                    ghost[v] = ghost[v] + cj * shifted(ring.at[1 - zone, v], (t + j) % 4096)
            for v in range(V):
                face[zone, n * V + v] = ghost[v]
            for k in range(KU - 1 - n):
                cur = [su[n, zone, v, k] for v in range(V)]
                th = [jnp.tanh(a) for a in cur]
                kk = sk[zone, k]
                for v in range(V):
                    outward = ghost[v] if k == 0 else su[n, zone, v, k - 1]
                    lap = rows_beside(cur[v]) + outward + su[n, zone, v, k + 1] - 4.0 * cur[v]
                    react = coup[v, 0] * th[0]
                    for w in range(1, V):
                        react = react + coup[v, w] * th[w]
                    su[n + 1, zone, v, k] = cur[v] + kk * lap - react
                    if k < n:
                        sd[n, zone, v, k] = 1.0 - th[v] * th[v]
            return carry

        lax.fori_loop(0, 2, step, 0)
        between(n)

    for n in (3, 2, 1, 0):
        m = 3 - n

        def taps(zone, carry):
            for v in range(V):
                put_ring(ring.at[zone, v], sk[zone, 0] * sl[m, zone, v, 0])
            return carry

        lax.fori_loop(0, 2, taps, 0)

        def back(zone, carry):
            other = 1 - zone
            acc = [jnp.zeros((32, 128), F32)] * V
            t = shift[other, n]
            for j in range(6):
                put_ring(tring, tap[other, n, j])
                amount = (8192 - t - j) % 4096
                cj = shifted(tring, amount)
                for v in range(V):
                    acc[v] = acc[v] + cj * shifted(ring.at[other, v], amount)
            for v in range(V):
                face[zone, 15 + n * V + v] = acc[v]
            for k in range(n):
                cur = [sl[m, zone, v, k] for v in range(V)]
                kk = sk[zone, k]
                for v in range(V):
                    s = kk * cur[v]
                    lap = rows_beside(s) + sk[zone, k + 1] * sl[m, zone, v, k + 1] - 4.0 * s
                    if k == 0:
                        lap = lap + acc[v]
                    else:
                        lap = lap + sk[zone, k - 1] * sl[m, zone, v, k - 1]
                    if n == 3:
                        th = jnp.tanh(su[3, zone, v, k])
                        d = 1.0 - th * th
                    else:
                        d = sd[n, zone, v, k]
                    pulled = coup[0, v] * cur[0]
                    for w in range(1, V):
                        pulled = pulled + coup[w, v] * cur[w]
                    sl[m + 1, zone, v, k] = cur[v] + lap - d * pulled
            return carry

        if n > 0:
            lax.fori_loop(0, 2, back, 0)
        else:
            back(q, 0)
        between(6 - n)


def face_columns(face, q, b, cols):
    pad = jnp.zeros((128 - 35, 128), F32)
    for part, dst, size, lo in (((b + 31) % 32, 8, 8, 120), (b, 16, 128, 0), ((b + 1) % 32, 144, 8, 0)):
        rows = face[q, pl.ds(part, 35, stride=32), :]
        cols[dst : dst + size, :] = jnp.concatenate([rows, pad], axis=0).T[lo : lo + size, :]


def scatter_points(hsum, area, proj, ids, dist, partial):
    lane = lane_of((128, 128))
    hs = [hsum[v, 16:144, :] for v in range(V)]
    acc = jnp.zeros((128, 128), F32)
    for c in range(3):
        col = proj[c, 0] * hs[0]
        for v in range(1, V):
            col = col + proj[c, v] * hs[v]
        acc = acc + jnp.where(lane == c, pltpu.roll(col, c, 1), 0.0)
    spread = (
        lax.broadcasted_iota(jnp.int32, (128, 384), 1) // 3 == lax.broadcasted_iota(jnp.int32, (128, 384), 0)
    ).astype(F32)
    sens = lax.dot_general(
        acc, spread, (((0,), (0,)), ((), ())), precision=lax.Precision.HIGHEST, preferred_element_type=F32
    )
    sens = [sens[c : c + 1, :] * area[...] for c in range(3)]
    sub_a = lax.broadcasted_iota(jnp.int32, (128, 128), 0)
    sub_b = lax.broadcasted_iota(jnp.int32, (256, 128), 0)
    total = jnp.zeros((384, 256), F32)
    for k in range(8):
        dk = dist[k : k + 1, :]
        om = 1.0 - dk
        om = om * om
        phi = om * om * (4.0 * dk + 1.0)
        idk = ids[k : k + 1, :]
        for wt in range(3):
            cut = slice(wt * 128, (wt + 1) * 128)
            idt = idk[:, cut]
            ch = idt // 256
            rowid = (ch % 2) * 64 + ((ch // 8) % 4) * 16 + ((ch // 2) % 4) * 4 + ch // 32
            mask = sub_a == rowid
            high, low = [], []
            for c in range(3):
                val = phi[:, cut] * sens[c][:, cut]
                hi = val.astype(jnp.bfloat16).astype(F32)
                high.append(jnp.where(mask, hi, 0.0).astype(jnp.bfloat16))
                low.append(jnp.where(mask, val - hi, 0.0).astype(jnp.bfloat16))
            left = jnp.concatenate([jnp.concatenate(high, axis=0), jnp.concatenate(low, axis=0)], axis=1)
            onehot = jnp.where(sub_b == idt % 256, 1.0, 0.0).astype(jnp.bfloat16)
            right = jnp.concatenate([onehot, onehot], axis=1)
            total = total + lax.dot_general(
                left, right, (((1,), (1,)), ((), ())), preferred_element_type=F32
            )
    for c in range(3):
        partial[c] = total[c * 128 : (c + 1) * 128, :]


def window_kernel(
    coup, proj, u_hbm, k_hbm, l_hbm, m_hbm, w_hbm, area, ids, dist, out_hbm, points,
    u0, u1, u2, u3, d0, d1, d2, l4, l3, l2, l1, s4, s3, s2, s1, kap, hsum, outv,
    su, sd, sl, sk, tap, ring, tring, face, cols, shift,
    gat, hu, hl, hk, chunk, mt, wt, partial, r1, q1, r2, q2, r3, q3, r4,
    sem, osem, halo_s, halo_r, first_s, first_r, ph_s, ph_r, core_s, core_r, rs_s, rs_r,
):
    y, b, x, z, c = place()
    q = y % 2
    yp = y + 1 - 2 * q
    b0 = b - c
    twin = b0 + 1 - c
    nxt, prv = (b + 1) % 32, (b + 31) % 32
    us, ds, ls, ss = (u0, u1, u2, u3), (d0, d1, d2), (l4, l3, l2, l1), (s4, s3, s2, s1)

    def loads_of(t):
        cut = pl.ds(t * 128, 128)
        own = pl.ds(16, 128)
        return [
            pltpu.make_async_copy(u_hbm.at[:, 0, :, cut], u0.at[:, t, own, :], sem.at[3 * t]),
            pltpu.make_async_copy(l_hbm.at[:, 0, :, cut], l4.at[:, t, own, :], sem.at[3 * t + 1]),
            pltpu.make_async_copy(k_hbm.at[0, :, cut], kap.at[t, own, :], sem.at[3 * t + 2]),
        ]

    mine = pl.ds(pl.multiple_of(b * 128, 128), 128)
    maps = [
        pltpu.make_async_copy(m_hbm.at[:, 0, mine], mt, sem.at[12]),
        pltpu.make_async_copy(w_hbm.at[:, 0, mine], wt, sem.at[13]),
    ]
    loads = [loads_of(t) for t in range(4)]
    for copy in loads[3] + maps + loads[0] + loads[1] + loads[2]:
        copy.start()

    barrier = pltpu.get_barrier_semaphore()
    peers = [(y, nxt), (y, prv), (yp, b0), (yp, b0 + 1), (y, twin)]
    for d in (1, 2, 3):
        peers.append((y, block_of((x + d) % 4, z, c)))
        peers.append((y, block_of(x, (z + d) % 4, c)))
        peers.append(((y + d) % 4, b))
    for peer in peers:
        pl.semaphore_signal(barrier, inc=1, device_id=peer, device_id_type=MESH)
    pl.semaphore_wait(barrier, len(peers))

    halo = []
    for n, (src, dst) in enumerate(((u_hbm, hu), (l_hbm, hl), (k_hbm, hk))):

        def rows(r):
            return src.at[:, 0, pl.ds(r, 8), :] if len(src.shape) == 4 else src.at[0, pl.ds(r, 8), :]

        halo.append(remote(rows(120), dst.at[0], halo_s.at[n], halo_r.at[n], y, nxt))
        halo.append(remote(rows(0), dst.at[1], halo_s.at[3 + n], halo_r.at[3 + n], y, prv))
    for copy in halo:
        copy.start()

    for copy in loads[3] + maps:
        copy.wait()
    for v in range(V):
        chunk[KU * v : KU * (v + 1), :] = u0[v, 3, 16:144, :].T[128 - KU :, :]
        chunk[OFF_L + KL * v : OFF_L + KL * (v + 1), :] = l4[v, 3, 16:144, :].T[128 - KL :, :]
    chunk[OFF_K : OFF_K + KU, :] = kap[3, 16:144, :].T[128 - KU :, :]
    chunk[OFF_M : OFF_M + 4, :] = mt[...].astype(F32)
    chunk[OFF_W : OFF_W + 4, :] = wt[...]

    here = gat.at[q, x, z * 2 + c]
    across = remote(chunk, here, first_s.at[0], first_r.at[c], yp, b0 + q)
    across.start()

    @pl.when(c == q)
    def _():
        gat[q, x, z * 2 + c] = chunk[...]

    @pl.when(c != q)
    def _():
        remote(chunk, here, first_s.at[1], first_r.at[2], y, b0 + q).start()

    def part(core, stage, d):
        if core == 0:
            if stage == 0:
                return gat.at[0, (x + d) % 4, pl.ds(z * 2, 2)]
            return gat.at[0, :, pl.ds((z + d) % 4 * 2, 2)]
        if stage == 0:
            return gat.at[1, x, pl.ds((z + d) % 4 * 2, 2)]
        return gat.at[1, (x + d) % 4]

    def hops(core, stage):
        copies = []
        for d in (1, 2, 3):
            to = block_of((x + d) % 4, z, c) if core == stage else block_of(x, (z + d) % 4, c)
            n = 3 * stage + d - 1
            copies.append(remote(part(core, stage, 0), part(core, stage, 0), ph_s.at[n], ph_r.at[n], y, to))
        return copies

    def swaps(core, whose):
        return [
            remote(part(whose, 1, d), part(whose, 1, d), core_s.at[d], core_r.at[d], y, twin) for d in range(4)
        ]

    def on_core(core, action):
        @pl.when(c == core)
        def _():
            action(core)

    def first_stage(core):
        @pl.when(q == core)
        def _():
            remote(chunk, here, first_s.at[1], first_r.at[2], y, b0 + q).wait_recv()

        @pl.when(q != core)
        def _():
            for j in range(2):
                remote(chunk, here, first_s.at[0], first_r.at[j], yp, b0 + q).wait_recv()

        for copy in hops(core, 0):
            copy.start()

    def second_stage(core):
        for copy in hops(core, 0):
            copy.wait()
        for copy in hops(core, 1):
            copy.start()
        swaps(core, core)[0].start()

    def third_stage(core):
        copies, sends = hops(core, 1), swaps(core, core)
        for copy in copies:
            copy.wait()
        for copy in sends[1:]:
            copy.start()

    def last_stage(core):
        for copy in swaps(core, core):
            copy.wait_send()
        for copy in swaps(core, 1 - core):
            copy.wait_recv()

    for core in range(2):
        on_core(core, first_stage)

    for copy in halo:
        copy.wait()
    for copy in loads[0] + loads[1] + loads[2]:
        copy.wait()
    for t in range(4):
        cut = slice(t * 128, (t + 1) * 128)
        for side, r in ((0, 8), (1, 144)):
            kap[t, r : r + 8, :] = hk[side, :, cut]
            for v in range(V):
                u0[v, t, r : r + 8, :] = hu[side, v, :, cut]
                l4[v, t, r : r + 8, :] = hl[side, v, :, cut]

    def scale(i):
        rows = pl.ds(pl.multiple_of(8 + i * 8, 8), 8)
        for t in range(4):
            k = kap[t, rows, :]
            for v in range(V):
                s4[v, t, rows, :] = k * l4[v, t, rows, :]

    over_rows(scale, 0, 18, 2)
    for core in range(2):
        on_core(core, second_stage)

    every = (0, 1, 2, 3)
    for n in range(3):
        main_forward(n, us, ds, kap, coup, every, None)
    for n in (3, 2, 1, 0):
        main_adjoint(n, us, ds, ls, ss, kap, coup, every, None, hsum, outv)

    for core in range(2):
        on_core(core, third_stage)

    scatter_points(hsum, area, proj, ids, dist, partial)
    first = remote(
        partial.at[:, pl.ds(pl.multiple_of((1 - c) * 64, 64), 64), :], r1, rs_s.at[0], rs_r.at[0], y, twin
    )
    first.start()
    for core in range(2):
        on_core(core, last_stage)
    across.wait_send()

    @pl.when(c != q)
    def _():
        remote(chunk, here, first_s.at[1], first_r.at[2], y, b0 + q).wait_send()

    def sent(slots, got, base, to_of):
        copies = []
        for d in (1, 2, 3):
            index, ty, tb = to_of(d)
            copies.append(
                remote(slots.at[index], got.at[d - 1], rs_s.at[base + d], rs_r.at[base + d], ty, tb)
            )
        return copies

    by_x = sent(q1, r2, 0, lambda d: ((x + d) % 4, y, block_of((x + d) % 4, z, c)))
    by_z = sent(q2, r3, 3, lambda d: ((z + d) % 4, y, block_of(x, (z + d) % 4, c)))
    by_y = sent(q3, r4, 6, lambda d: ((y + d) % 4, (y + d) % 4, b))

    def between(step):
        if step == 0:
            first.wait()
            own = pl.multiple_of(c * 64, 64)
            for j in range(4):
                q1[j] = partial[:, pl.ds(own + j * 16, 16), :] + r1[:, j * 16 : (j + 1) * 16, :]
            for copy in by_x:
                copy.start()
        if step == 2:
            for copy in by_x:
                copy.wait()
            total = q1[x] + r2[0] + r2[1] + r2[2]
            for j in range(4):
                q2[j] = total[:, j * 4 : (j + 1) * 4, :]
            for copy in by_z:
                copy.start()
        if step == 4:
            for copy in by_z:
                copy.wait()
            total = q2[z] + r3[0] + r3[1] + r3[2]
            for j in range(4):
                q3[j] = total[:, j, :]
            for copy in by_y:
                copy.start()

    strips(gat.reshape(2, 32 * CHUNK, 128), q, coup, su, sd, sl, sk, tap, shift, ring, tring, face, between)
    for copy in by_y:
        copy.wait()
    points[...] = q3[y] + r4[0] + r4[1] + r4[2]

    face_columns(face.reshape(2, 35 * 32, 128), q, b, cols)
    stores = [
        pltpu.make_async_copy(outv.at[:, t], out_hbm.at[:, 0, :, pl.ds(t * 128, 128)], osem.at[t])
        for t in range(4)
    ]
    for copy in stores[:3]:
        copy.start()
    for n in range(3):
        main_forward(n, us, ds, kap, coup, (3,), cols)
    for n in (3, 2, 1, 0):
        main_adjoint(n, us, ds, ls, ss, kap, coup, (3,), cols, None, outv)
    stores[3].start()
    for copy in stores:
        copy.wait()


def local(
    start_state, diffusivity, donor_map, donor_weight, coupling, final_cotangent,
    wall_area, wall_projection, center_ids, center_dist,
):
    any_ = pl.BlockSpec(memory_space=pl.ANY)
    vmem = pl.BlockSpec(memory_space=pltpu.VMEM)
    smem = pl.BlockSpec(memory_space=pltpu.SMEM)
    dma = pltpu.SemaphoreType.DMA

    def buf(*shape, dtype=F32):
        return pltpu.VMEM(shape, dtype)

    return pl.pallas_call(
        window_kernel,
        out_shape=(jax.ShapeDtypeStruct((V, 1, 128, 512), F32), jax.ShapeDtypeStruct((3, 256), F32)),
        in_specs=[smem, smem, any_, any_, any_, any_, any_, vmem, vmem, vmem],
        out_specs=(any_, vmem),
        scratch_shapes=[buf(V, 4, ROWS, 128)] * 15
        + [
            buf(4, ROWS, 128),
            buf(V, ROWS, 128),
            buf(V, 4, 128, 128),
            buf(4, 2, V, KU, 32, 128),
            buf(3, 2, V, 2, 32, 128),
            buf(4, 2, V, KL, 32, 128),
            buf(2, KU, 32, 128),
            buf(2, 4, 6, 32, 128),
            buf(2, V, 72, 128),
            buf(72, 128),
            buf(2, 35, 32, 128),
            buf(ROWS, 128),
            pltpu.SMEM((2, 4), jnp.int32),
            buf(2, 4, 8, CHUNK, 128),
            buf(2, V, 8, 512),
            buf(2, V, 8, 512),
            buf(2, 8, 512),
            buf(CHUNK, 128),
            buf(4, 128, dtype=jnp.int32),
            buf(4, 128),
            buf(3, 128, 256),
            buf(3, 64, 256),
            buf(4, 3, 16, 256),
            buf(3, 3, 16, 256),
            buf(4, 3, 4, 256),
            buf(3, 3, 4, 256),
            buf(4, 3, 256),
            buf(3, 3, 256),
        ]
        + [dma((n,)) for n in (14, 4, 6, 6, 2, 3, 6, 6, 4, 4, 10, 10)],
        compiler_params=pltpu.CompilerParams(
            collective_id=0, has_side_effects=True, vmem_limit_bytes=60 * 1024 * 1024
        ),
        name="window",
    )(
        coupling, wall_projection, start_state, diffusivity, final_cotangent, donor_map, donor_weight,
        wall_area, center_ids[0], center_dist[0],
    )


def solution(mesh):
    return jax.shard_map(
        local,
        mesh=mesh,
        in_specs=(
            P(None, "zone", "block", None),
            P("zone", "block", None),
            P(None, "zone", None),
            P(None, "zone", None),
            P(),
            P(None, "zone", "block", None),
            P("zone", "block"),
            P(),
            P("zone", None, "block"),
            P("zone", None, "block"),
        ),
        out_specs=(P(None, "zone", "block", None), P(None, ("zone", "block"))),
        check_vma=False,
    )
```

```python
import functools

import jax
import jax.numpy as jnp
from jax import lax
from jax.experimental import pallas as pl
from jax.experimental.pallas import tpu as pltpu
from jax.sharding import PartitionSpec as P

MESH = pl.DeviceIdType.MESH
F32 = jnp.float32
V = 5
KU = 6
KL = 4
OFF_L = V * KU
OFF_K = OFF_L + V * KL
OFF_M = OFF_K + KU
OFF_W = OFF_M + 4
CHUNK = 64
ROWS = 160


def lane_of(shape):
    return lax.broadcasted_iota(jnp.int32, shape, len(shape) - 1)


def place():
    y = lax.axis_index("zone")
    b = lax.axis_index("block")
    return y, b, b // 8, (b // 2) % 4, b % 2


def block_of(x, z, c):
    return x * 8 + z * 2 + c


def remote(src, dst, send, recv, y, b):
    return pltpu.make_async_remote_copy(
        src_ref=src, dst_ref=dst, send_sem=send, recv_sem=recv, device_id=(y, b), device_id_type=MESH
    )


def over_rows(body, first, count, unroll):
    def several(i, carry):
        for j in range(unroll):
            body(first + i * unroll + j)
        return carry

    lax.fori_loop(0, count // unroll, several, 0)


def over_edges(body, count):
    def side(i, carry):
        for j in range(count):
            body(i * (18 - count) + j)
        return carry

    lax.fori_loop(0, 2, side, 0)


def main_forward(n, us, ds, kap, kc, coup, tiles, ghost, where):
    lane = lane_of((8, 128))
    cf = [[coup[v, w] for w in range(V)] for v in range(V)]
    src, dst, dd = us[n], us[n + 1], ds[n]

    def body(i):
        r = pl.multiple_of(8 + i * 8, 8)
        rows = pl.ds(r, 8)
        for t in tiles:
            k = kap[t, rows, :]
            a = kc[t, rows, :]
            cur = [src[v, t, rows, :] for v in range(V)]
            th = [jnp.tanh(e) for e in cur]
            for v in range(V):
                if t == 0:
                    left = jnp.where(lane == 127, 0.0, cur[v])
                else:
                    left = jnp.where(lane == 127, src[v, t - 1, rows, :], cur[v])
                if t < 3:
                    right = jnp.where(lane == 0, src[v, t + 1, rows, :], cur[v])
                elif ghost is None:
                    right = jnp.where(lane == 0, 0.0, cur[v])
                else:
                    g = pltpu.roll(ghost[rows, :], (128 - (n * V + v)) % 128, 1)
                    right = jnp.where(lane == 0, g, cur[v])
                lap = (
                    src[v, t, pl.ds(r - 1, 8), :] + src[v, t, pl.ds(r + 1, 8), :]
                    + pltpu.roll(left, 1, 1) + pltpu.roll(right, 127, 1)
                )
                react = cf[v][0] * th[0]
                for w in range(1, V):
                    react = react + cf[v][w] * th[w]
                dst[v, t, rows, :] = a * cur[v] + k * lap - react
                dd[v, t, rows, :] = 1.0 - th[v] * th[v]

    where(body)


def inner(margin):
    return lambda body: over_rows(body, margin, 18 - 2 * margin, 2)


def edges(count):
    return lambda body: over_edges(body, count)


def all_rows(body):
    over_rows(body, 0, 18, 6)


def main_adjoint(n, us, ds, ls, ss, kap, kc, coup, tiles, back, hsum, out):
    lane = lane_of((8, 128))
    cf = [[coup[w, v] for w in range(V)] for v in range(V)]
    m = 3 - n
    lam, sca = ls[m], ss[m]

    def body(i):
        r = pl.multiple_of(8 + i * 8, 8)
        rows = pl.ds(r, 8)
        for t in tiles:
            cur = [lam[v, t, rows, :] for v in range(V)]
            a = kc[t, rows, :]
            for v in range(V):
                s = sca[v, t, rows, :]
                if t == 0:
                    left = jnp.where(lane == 127, 0.0, s)
                else:
                    left = jnp.where(lane == 127, sca[v, t - 1, rows, :], s)
                right = jnp.where(lane == 0, sca[v, t + 1, rows, :] if t < 3 else 0.0, s)
                lap = (
                    sca[v, t, pl.ds(r - 1, 8), :] + sca[v, t, pl.ds(r + 1, 8), :]
                    + pltpu.roll(left, 1, 1) + pltpu.roll(right, 127, 1)
                )
                if n == 3:
                    th = jnp.tanh(us[3][v, t, rows, :])
                    d = 1.0 - th * th
                else:
                    d = ds[n][v, t, rows, :]
                pulled = cf[v][0] * cur[0]
                for w in range(1, V):
                    pulled = pulled + cf[v][w] * cur[w]
                new = a * cur[v] + lap - d * pulled
                if t == 3 and back is not None:
                    f = pltpu.roll(back[rows, :], 127 - (15 + n * V + v), 1)
                    new = new + jnp.where(lane == 127, f, 0.0)
                if n > 0:
                    ls[m + 1][v, t, rows, :] = new
                    ss[m + 1][v, t, rows, :] = kap[t, rows, :] * new
                else:
                    out[v, t, pl.ds(pl.multiple_of(r - 16, 8), 8), :] = new
                if t == 0 and hsum is not None:
                    p = cur[v] * us[n][v, t, rows, :]
                    if n == 3:
                        hsum[v, rows, :] = p
                    else:
                        hsum[v, rows, :] = hsum[v, rows, :] + p

    if n > 0:
        over_rows(body, 0, 18, 6 if len(tiles) == 1 else 2)
    else:
        over_rows(body, 1, 16, 4 if len(tiles) == 1 else 2)


def rows_beside(a):
    lane = lane_of(a.shape)
    up = pltpu.roll(jnp.where(lane == 127, pltpu.roll(a, 1, 0), a), 1, 1)
    down = pltpu.roll(jnp.where(lane == 0, pltpu.roll(a, 31, 0), a), 127, 1)
    return up + down


def put_ring(ring, a):
    ring[0:32, :] = a
    ring[32:64, :] = a
    ring[64:72, :] = a[0:8]


def shifted(ring, amount):
    lane = lane_of((32, 128))
    high, low = amount // 128, amount % 128
    first = ring[pl.ds(high, 32), :]
    second = ring[pl.ds(high + 1, 32), :]
    return pltpu.roll(jnp.where(lane < low, second, first), (128 - low) % 128, 1)


def strips(gat, q, coup, su, sd, sl, sk, tap, shift, ring, tring, face):
    row = lax.broadcasted_iota(jnp.int32, (32, 128), 0) * 128 + lane_of((32, 128))

    def get(zone, j):
        return gat[zone, pl.ds(j, 32, stride=CHUNK), :]

    def unpack(zone, carry):
        for v in range(V):
            for k in range(KU):
                su[0, zone, v, k] = get(zone, v * KU + KU - 1 - k)
            for k in range(KL):
                sl[0, zone, v, k] = get(zone, OFF_L + v * KL + KL - 1 - k)
        for k in range(KU):
            sk[zone, k] = get(zone, OFF_K + KU - 1 - k)
        for n in range(4):
            d = get(zone, OFF_M + n).astype(jnp.int32) - row
            base = d[0:1, 0:1]
            d = d - base
            d = jnp.where(d > 2048, d - 4096, d)
            d = jnp.where(d > 2048, d - 4096, d)
            d = jnp.where(d < -2048, d + 4096, d)
            d = jnp.where(d < -2048, d + 4096, d)
            least = jnp.min(d)
            e = d - least
            w = get(zone, OFF_W + n)
            shift[zone, n] = (base[0, 0] + least + 8192) % 4096
            for j in range(6):
                tap[zone, n, j] = jnp.where(e == j, w, 0.0) + jnp.where(e == j - 1, 1.0 - w, 0.0)
        return carry

    lax.fori_loop(0, 2, unpack, 0)

    for n in range(3):
        def faces(zone, carry):
            for v in range(V):
                put_ring(ring.at[zone, v], su[n, zone, v, 0])
            return carry

        lax.fori_loop(0, 2, faces, 0)

        def step(zone, carry):
            ghost = [jnp.zeros((32, 128), F32)] * V
            t = shift[zone, n]
            for j in range(6):
                cj = tap[zone, n, j]
                for v in range(V):
                    ghost[v] = ghost[v] + cj * shifted(ring.at[1 - zone, v], (t + j) % 4096)
            for v in range(V):
                face[zone, n * V + v] = ghost[v]
            for k in range(KU - 1 - n):
                cur = [su[n, zone, v, k] for v in range(V)]
                th = [jnp.tanh(a) for a in cur]
                kk = sk[zone, k]
                for v in range(V):
                    outward = ghost[v] if k == 0 else su[n, zone, v, k - 1]
                    lap = rows_beside(cur[v]) + outward + su[n, zone, v, k + 1] - 4.0 * cur[v]
                    react = coup[v, 0] * th[0]
                    for w in range(1, V):
                        react = react + coup[v, w] * th[w]
                    su[n + 1, zone, v, k] = cur[v] + kk * lap - react
                    if k < n:
                        sd[n, zone, v, k] = 1.0 - th[v] * th[v]
            return carry

        lax.fori_loop(0, 2, step, 0)

    for n in (3, 2, 1, 0):
        m = 3 - n

        def taps(zone, carry):
            for v in range(V):
                put_ring(ring.at[zone, v], sk[zone, 0] * sl[m, zone, v, 0])
            return carry

        lax.fori_loop(0, 2, taps, 0)

        def back(zone, carry):
            other = 1 - zone
            acc = [jnp.zeros((32, 128), F32)] * V
            t = shift[other, n]
            for j in range(6):
                put_ring(tring, tap[other, n, j])
                amount = (8192 - t - j) % 4096
                cj = shifted(tring, amount)
                for v in range(V):
                    acc[v] = acc[v] + cj * shifted(ring.at[other, v], amount)
            for v in range(V):
                face[zone, 15 + n * V + v] = acc[v]
            for k in range(n):
                cur = [sl[m, zone, v, k] for v in range(V)]
                kk = sk[zone, k]
                for v in range(V):
                    s = kk * cur[v]
                    lap = rows_beside(s) + sk[zone, k + 1] * sl[m, zone, v, k + 1] - 4.0 * s
                    if k == 0:
                        lap = lap + acc[v]
                    else:
                        lap = lap + sk[zone, k - 1] * sl[m, zone, v, k - 1]
                    if n == 3:
                        th = jnp.tanh(su[3, zone, v, k])
                        d = 1.0 - th * th
                    else:
                        d = sd[n, zone, v, k]
                    pulled = coup[0, v] * cur[0]
                    for w in range(1, V):
                        pulled = pulled + coup[w, v] * cur[w]
                    sl[m + 1, zone, v, k] = cur[v] + lap - d * pulled
            return carry

        if n > 0:
            lax.fori_loop(0, 2, back, 0)
        else:
            back(q, 0)


def face_columns(face, q, b, cols):
    pad = jnp.zeros((128 - 35, 128), F32)
    for part, dst, size, lo in (((b + 31) % 32, 8, 8, 120), (b, 16, 128, 0), ((b + 1) % 32, 144, 8, 0)):
        rows = face[q, pl.ds(part, 35, stride=32), :]
        cols[dst : dst + size, :] = jnp.concatenate([rows, pad], axis=0).T[lo : lo + size, :]


def scatter_points(hsum, l1, u0, area, proj, ids, dist, partial):
    lane = lane_of((128, 128))
    hs = [hsum[v, 16:144, :] + l1[v, 0, 16:144, :] * u0[v, 0, 16:144, :] for v in range(V)]
    acc = jnp.zeros((128, 128), F32)
    for c in range(3):
        col = proj[c, 0] * hs[0]
        for v in range(1, V):
            col = col + proj[c, v] * hs[v]
        acc = acc + jnp.where(lane == c, pltpu.roll(col, c, 1), 0.0)
    spread = (
        lax.broadcasted_iota(jnp.int32, (128, 384), 1) // 3 == lax.broadcasted_iota(jnp.int32, (128, 384), 0)
    ).astype(F32)
    sens = lax.dot_general(
        acc, spread, (((0,), (0,)), ((), ())), precision=lax.Precision.HIGHEST, preferred_element_type=F32
    )
    sens = [sens[c : c + 1, :] * area[...] for c in range(3)]
    sub_a = lax.broadcasted_iota(jnp.int32, (128, 128), 0)
    sub_b = lax.broadcasted_iota(jnp.int32, (256, 128), 0)
    total = jnp.zeros((384, 256), F32)
    for k in range(8):
        dk = dist[k : k + 1, :]
        om = 1.0 - dk
        om = om * om
        phi = om * om * (4.0 * dk + 1.0)
        idk = ids[k : k + 1, :]
        for wt in range(3):
            cut = slice(wt * 128, (wt + 1) * 128)
            idt = idk[:, cut]
            ch = idt // 256
            rowid = (ch % 2) * 64 + ((ch // 8) % 4) * 16 + ((ch // 2) % 4) * 4 + ch // 32
            mask = sub_a == rowid
            high, low = [], []
            for c in range(3):
                val = phi[:, cut] * sens[c][:, cut]
                hi = val.astype(jnp.bfloat16).astype(F32)
                high.append(jnp.where(mask, hi, 0.0).astype(jnp.bfloat16))
                low.append(jnp.where(mask, val - hi, 0.0).astype(jnp.bfloat16))
            left = jnp.concatenate([jnp.concatenate(high, axis=0), jnp.concatenate(low, axis=0)], axis=1)
            onehot = jnp.where(sub_b == idt % 256, 1.0, 0.0).astype(jnp.bfloat16)
            right = jnp.concatenate([onehot, onehot], axis=1)
            total = total + lax.dot_general(
                left, right, (((1,), (1,)), ((), ())), preferred_element_type=F32
            )
    for c in range(3):
        partial[c] = total[c * 128 : (c + 1) * 128, :]


def window_kernel(
    coup, proj, u_hbm, k_hbm, l_hbm, m_hbm, w_hbm, area, ids, dist, out_hbm, points,
    u0, u1, u2, u3, d0, d1, d2, l4, l3, l2, l1, s4, s3, s2, s1, kap, kc, hsum, outv,
    su, sd, sl, sk, tap, ring, tring, face, cols, shift,
    gat, hu, hl, hk, chunk, mt, wt, partial, r1, q1, r2, q2, r3, q3, r4,
    sem, osem, halo_s, halo_r, first_s, first_r, ph_s, ph_r, core_s, core_r, rs_s, rs_r,
):
    y, b, x, z, c = place()
    q = y % 2
    yp = y + 1 - 2 * q
    b0 = b - c
    twin = b0 + 1 - c
    nxt, prv = (b + 1) % 32, (b + 31) % 32
    us, ds, ls, ss = (u0, u1, u2, u3), (d0, d1, d2), (l4, l3, l2, l1), (s4, s3, s2, s1)

    def loads_of(t):
        cut = pl.ds(t * 128, 128)
        own = pl.ds(16, 128)
        return [
            pltpu.make_async_copy(u_hbm.at[:, 0, :, cut], u0.at[:, t, own, :], sem.at[3 * t]),
            pltpu.make_async_copy(l_hbm.at[:, 0, :, cut], l4.at[:, t, own, :], sem.at[3 * t + 1]),
            pltpu.make_async_copy(k_hbm.at[0, :, cut], kap.at[t, own, :], sem.at[3 * t + 2]),
        ]

    mine = pl.ds(pl.multiple_of(b * 128, 128), 128)
    maps = [
        pltpu.make_async_copy(m_hbm.at[:, 0, mine], mt, sem.at[12]),
        pltpu.make_async_copy(w_hbm.at[:, 0, mine], wt, sem.at[13]),
    ]
    loads = [loads_of(t) for t in range(4)]
    for copy in loads[3] + maps + loads[0] + loads[1] + loads[2]:
        copy.start()

    barrier = pltpu.get_barrier_semaphore()
    peers = [(y, nxt), (y, prv), (yp, b0), (yp, b0 + 1), (y, twin)]
    for d in (1, 2, 3):
        peers.append((y, block_of((x + d) % 4, z, c)))
        peers.append((y, block_of(x, (z + d) % 4, c)))
        peers.append(((y + d) % 4, b))
    for peer in peers:
        pl.semaphore_signal(barrier, inc=1, device_id=peer, device_id_type=MESH)

    halo = []
    for n, (src, dst) in enumerate(((u_hbm, hu), (l_hbm, hl), (k_hbm, hk))):

        def rows(r):
            return src.at[:, 0, pl.ds(r, 8), :] if len(src.shape) == 4 else src.at[0, pl.ds(r, 8), :]

        halo.append(remote(rows(120), dst.at[0], halo_s.at[n], halo_r.at[n], y, nxt))
        halo.append(remote(rows(0), dst.at[1], halo_s.at[3 + n], halo_r.at[3 + n], y, prv))

    for copy in loads[3] + maps:
        copy.wait()
    for v in range(V):
        chunk[KU * v : KU * (v + 1), :] = u0[v, 3, 16:144, :].T[128 - KU :, :]
        chunk[OFF_L + KL * v : OFF_L + KL * (v + 1), :] = l4[v, 3, 16:144, :].T[128 - KL :, :]
    chunk[OFF_K : OFF_K + KU, :] = kap[3, 16:144, :].T[128 - KU :, :]
    chunk[OFF_M : OFF_M + 4, :] = mt[...].astype(F32)
    chunk[OFF_W : OFF_W + 4, :] = wt[...]

    for copy in loads[0] + loads[1] + loads[2]:
        copy.wait()

    def scale(i):
        rows = pl.ds(pl.multiple_of(8 + i * 8, 8), 8)
        for t in range(4):
            k = kap[t, rows, :]
            kc[t, rows, :] = 1.0 - 4.0 * k
            for v in range(V):
                s4[v, t, rows, :] = k * l4[v, t, rows, :]

    every = (0, 1, 2, 3)
    over_rows(scale, 1, 16, 2)
    main_forward(0, us, ds, kap, kc, coup, every, None, inner(2))
    pl.semaphore_wait(barrier, len(peers))

    here = gat.at[q, x, z * 2 + c]
    across = remote(chunk, here, first_s.at[0], first_r.at[c], yp, b0 + q)
    across.start()
    for copy in halo:
        copy.start()

    @pl.when(c == q)
    def _():
        gat[q, x, z * 2 + c] = chunk[...]

    @pl.when(c != q)
    def _():
        remote(chunk, here, first_s.at[1], first_r.at[2], y, b0 + q).start()

    def part(core, stage, d):
        if core == 0:
            if stage == 0:
                return gat.at[0, (x + d) % 4, pl.ds(z * 2, 2)]
            return gat.at[0, :, pl.ds((z + d) % 4 * 2, 2)]
        if stage == 0:
            return gat.at[1, x, pl.ds((z + d) % 4 * 2, 2)]
        return gat.at[1, (x + d) % 4]

    def hops(core, stage):
        copies = []
        for d in (1, 2, 3):
            to = block_of((x + d) % 4, z, c) if core == stage else block_of(x, (z + d) % 4, c)
            n = 3 * stage + d - 1
            copies.append(remote(part(core, stage, 0), part(core, stage, 0), ph_s.at[n], ph_r.at[n], y, to))
        return copies

    def swaps(core, whose):
        return [
            remote(part(whose, 1, d), part(whose, 1, d), core_s.at[d], core_r.at[d], y, twin) for d in range(4)
        ]

    def on_core(core, action):
        @pl.when(c == core)
        def _():
            action(core)

    def first_stage(core):
        @pl.when(q == core)
        def _():
            remote(chunk, here, first_s.at[1], first_r.at[2], y, b0 + q).wait_recv()

        @pl.when(q != core)
        def _():
            for j in range(2):
                remote(chunk, here, first_s.at[0], first_r.at[j], yp, b0 + q).wait_recv()

        for copy in hops(core, 0):
            copy.start()

    def second_stage(core):
        for copy in hops(core, 0):
            copy.wait()
        for copy in hops(core, 1):
            copy.start()
        swaps(core, core)[0].start()

    def third_stage(core):
        copies, sends = hops(core, 1), swaps(core, core)
        for copy in copies:
            copy.wait()
        for copy in sends[1:]:
            copy.start()

    def last_stage(core):
        for copy in swaps(core, core):
            copy.wait_send()
        for copy in swaps(core, 1 - core):
            copy.wait_recv()

    main_forward(1, us, ds, kap, kc, coup, every, None, inner(3))
    for core in range(2):
        on_core(core, first_stage)
    main_forward(2, us, ds, kap, kc, coup, every, None, inner(4))

    for copy in halo:
        copy.wait()
    for t in range(4):
        cut = slice(t * 128, (t + 1) * 128)
        for side, r in ((0, 8), (1, 144)):
            kap[t, r : r + 8, :] = hk[side, :, cut]
            for v in range(V):
                u0[v, t, r : r + 8, :] = hu[side, v, :, cut]
                l4[v, t, r : r + 8, :] = hl[side, v, :, cut]

    over_edges(scale, 1)
    for n in range(3):
        main_forward(n, us, ds, kap, kc, coup, every, None, edges(n + 2))
    for core in range(2):
        on_core(core, second_stage)

    for n in (3, 2, 1):
        main_adjoint(n, us, ds, ls, ss, kap, kc, coup, (0,), None, hsum, outv)
    scatter_points(hsum, l1, u0, area, proj, ids, dist, partial)
    first = remote(
        partial.at[:, pl.ds(pl.multiple_of((1 - c) * 64, 64), 64), :], r1, rs_s.at[0], rs_r.at[0], y, twin
    )
    first.start()

    def sent(slots, got, base, to_of):
        copies = []
        for d in (1, 2, 3):
            index, ty, tb = to_of(d)
            copies.append(
                remote(slots.at[index], got.at[d - 1], rs_s.at[base + d], rs_r.at[base + d], ty, tb)
            )
        return copies

    by_x = sent(q1, r2, 0, lambda d: ((x + d) % 4, y, block_of((x + d) % 4, z, c)))
    by_z = sent(q2, r3, 3, lambda d: ((z + d) % 4, y, block_of(x, (z + d) % 4, c)))
    by_y = sent(q3, r4, 6, lambda d: ((y + d) % 4, (y + d) % 4, b))

    def reduce_stage(step):
        if step == 0:
            first.wait()
            own = pl.multiple_of(c * 64, 64)
            for j in range(4):
                q1[j] = partial[:, pl.ds(own + j * 16, 16), :] + r1[:, j * 16 : (j + 1) * 16, :]
            for copy in by_x:
                copy.start()
        if step == 1:
            for copy in by_x:
                copy.wait()
            total = q1[x] + r2[0] + r2[1] + r2[2]
            for j in range(4):
                q2[j] = total[:, j * 4 : (j + 1) * 4, :]
            for copy in by_z:
                copy.start()
        if step == 2:
            for copy in by_z:
                copy.wait()
            total = q2[z] + r3[0] + r3[1] + r3[2]
            for j in range(4):
                q3[j] = total[:, j, :]
            for copy in by_y:
                copy.start()
        if step == 3:
            for copy in by_y:
                copy.wait()
            points[...] = q3[y] + r4[0] + r4[1] + r4[2]

    for n in (3, 2, 1, 0):
        main_adjoint(n, us, ds, ls, ss, kap, kc, coup, every, None, None, outv)
        reduce_stage(3 - n)
        if n == 2:
            for core in range(2):
                on_core(core, third_stage)
    for core in range(2):
        on_core(core, last_stage)
    across.wait_send()

    @pl.when(c != q)
    def _():
        remote(chunk, here, first_s.at[1], first_r.at[2], y, b0 + q).wait_send()

    strips(gat.reshape(2, 32 * CHUNK, 128), q, coup, su, sd, sl, sk, tap, shift, ring, tring, face)
    face_columns(face.reshape(2, 35 * 32, 128), q, b, cols)
    stores = [
        pltpu.make_async_copy(outv.at[:, t], out_hbm.at[:, 0, :, pl.ds(t * 128, 128)], osem.at[t])
        for t in range(4)
    ]
    for copy in stores[:3]:
        copy.start()
    for n in range(3):
        main_forward(n, us, ds, kap, kc, coup, (3,), cols, all_rows)
    for n in (3, 2, 1, 0):
        main_adjoint(n, us, ds, ls, ss, kap, kc, coup, (3,), cols, None, outv)
    stores[3].start()
    for copy in stores:
        copy.wait()


def local(
    start_state, diffusivity, donor_map, donor_weight, coupling, final_cotangent,
    wall_area, wall_projection, center_ids, center_dist,
):
    any_ = pl.BlockSpec(memory_space=pl.ANY)
    vmem = pl.BlockSpec(memory_space=pltpu.VMEM)
    smem = pl.BlockSpec(memory_space=pltpu.SMEM)
    dma = pltpu.SemaphoreType.DMA

    def buf(*shape, dtype=F32):
        return pltpu.VMEM(shape, dtype)

    return pl.pallas_call(
        window_kernel,
        out_shape=(jax.ShapeDtypeStruct((V, 1, 128, 512), F32), jax.ShapeDtypeStruct((3, 256), F32)),
        in_specs=[smem, smem, any_, any_, any_, any_, any_, vmem, vmem, vmem],
        out_specs=(any_, vmem),
        scratch_shapes=[buf(V, 4, ROWS, 128)] * 15
        + [
            buf(4, ROWS, 128),
            buf(4, ROWS, 128),
            buf(V, ROWS, 128),
            buf(V, 4, 128, 128),
            buf(4, 2, V, KU, 32, 128),
            buf(3, 2, V, 2, 32, 128),
            buf(4, 2, V, KL, 32, 128),
            buf(2, KU, 32, 128),
            buf(2, 4, 6, 32, 128),
            buf(2, V, 72, 128),
            buf(72, 128),
            buf(2, 35, 32, 128),
            buf(ROWS, 128),
            pltpu.SMEM((2, 4), jnp.int32),
            buf(2, 4, 8, CHUNK, 128),
            buf(2, V, 8, 512),
            buf(2, V, 8, 512),
            buf(2, 8, 512),
            buf(CHUNK, 128),
            buf(4, 128, dtype=jnp.int32),
            buf(4, 128),
            buf(3, 128, 256),
            buf(3, 64, 256),
            buf(4, 3, 16, 256),
            buf(3, 3, 16, 256),
            buf(4, 3, 4, 256),
            buf(3, 3, 4, 256),
            buf(4, 3, 256),
            buf(3, 3, 256),
        ]
        + [dma((n,)) for n in (14, 4, 6, 6, 2, 3, 6, 6, 4, 4, 10, 10)],
        compiler_params=pltpu.CompilerParams(
            collective_id=0, has_side_effects=True, vmem_limit_bytes=60 * 1024 * 1024
        ),
        name="window",
    )(
        coupling, wall_projection, start_state, diffusivity, final_cotangent, donor_map, donor_weight,
        wall_area, center_ids[0], center_dist[0],
    )


def solution(mesh):
    return jax.shard_map(
        local,
        mesh=mesh,
        in_specs=(
            P(None, "zone", "block", None),
            P("zone", "block", None),
            P(None, "zone", None),
            P(None, "zone", None),
            P(),
            P(None, "zone", "block", None),
            P("zone", "block"),
            P(),
            P("zone", None, "block"),
            P("zone", None, "block"),
        ),
        out_specs=(P(None, "zone", "block", None), P(None, ("zone", "block"))),
        check_vma=False,
    )
```

```python
import functools

import jax
import jax.numpy as jnp
from jax import lax
from jax.experimental import pallas as pl
from jax.experimental.pallas import tpu as pltpu
from jax.sharding import PartitionSpec as P

MESH = pl.DeviceIdType.MESH
F32 = jnp.float32
V = 5
KU = 6
KL = 4
OFF_L = V * KU
OFF_K = OFF_L + V * KL
OFF_M = OFF_K + KU
OFF_W = OFF_M + 4
CHUNK = 64
ROWS = 160


def lane_of(shape):
    return lax.broadcasted_iota(jnp.int32, shape, len(shape) - 1)


def place():
    y = lax.axis_index("zone")
    b = lax.axis_index("block")
    return y, b, b // 8, (b // 2) % 4, b % 2


def block_of(x, z, c):
    return x * 8 + z * 2 + c


def remote(src, dst, send, recv, y, b):
    return pltpu.make_async_remote_copy(
        src_ref=src, dst_ref=dst, send_sem=send, recv_sem=recv, device_id=(y, b), device_id_type=MESH
    )


def over_rows(body, first, count, unroll):
    def several(i, carry):
        for j in range(unroll):
            body(first + i * unroll + j)
        return carry

    lax.fori_loop(0, count // unroll, several, 0)


def over_edges(body, count):
    def side(i, carry):
        for j in range(count):
            body(i * (18 - count) + j)
        return carry

    lax.fori_loop(0, 2, side, 0)


def main_forward(n, us, ds, kap, kc, coup, tiles, ghost, where):
    lane = lane_of((8, 128))
    cf = [[coup[v, w] for w in range(V)] for v in range(V)]
    src, dst, dd = us[n], us[n + 1], ds[n]

    def body(i):
        r = pl.multiple_of(8 + i * 8, 8)
        rows = pl.ds(r, 8)
        for t in tiles:
            k = kap[t, rows, :]
            a = kc[t, rows, :]
            cur = [src[v, t, rows, :] for v in range(V)]
            th = [jnp.tanh(e) for e in cur]
            for v in range(V):
                if t == 0:
                    left = jnp.where(lane == 127, 0.0, cur[v])
                else:
                    left = jnp.where(lane == 127, src[v, t - 1, rows, :], cur[v])
                if t < 3:
                    right = jnp.where(lane == 0, src[v, t + 1, rows, :], cur[v])
                elif ghost is None:
                    right = jnp.where(lane == 0, 0.0, cur[v])
                else:
                    g = pltpu.roll(ghost[rows, :], (128 - (n * V + v)) % 128, 1)
                    right = jnp.where(lane == 0, g, cur[v])
                lap = (
                    src[v, t, pl.ds(r - 1, 8), :] + src[v, t, pl.ds(r + 1, 8), :]
                    + pltpu.roll(left, 1, 1) + pltpu.roll(right, 127, 1)
                )
                react = cf[v][0] * th[0]
                for w in range(1, V):
                    react = react + cf[v][w] * th[w]
                dst[v, t, rows, :] = a * cur[v] + k * lap - react
                dd[v, t, rows, :] = 1.0 - th[v] * th[v]

    where(body)


def inner(margin):
    return lambda body: over_rows(body, margin, 18 - 2 * margin, 2)


def edges(count):
    return lambda body: over_edges(body, count)


def all_rows(body):
    over_rows(body, 0, 18, 6)


def main_adjoint(n, us, ds, ls, ss, kap, kc, coup, tiles, back, hsum, out):
    lane = lane_of((8, 128))
    cf = [[coup[w, v] for w in range(V)] for v in range(V)]
    m = 3 - n
    lam, sca = ls[m], ss[m]

    def body(i):
        r = pl.multiple_of(8 + i * 8, 8)
        rows = pl.ds(r, 8)
        for t in tiles:
            cur = [lam[v, t, rows, :] for v in range(V)]
            a = kc[t, rows, :]
            for v in range(V):
                s = sca[v, t, rows, :]
                if t == 0:
                    left = jnp.where(lane == 127, 0.0, s)
                else:
                    left = jnp.where(lane == 127, sca[v, t - 1, rows, :], s)
                right = jnp.where(lane == 0, sca[v, t + 1, rows, :] if t < 3 else 0.0, s)
                lap = (
                    sca[v, t, pl.ds(r - 1, 8), :] + sca[v, t, pl.ds(r + 1, 8), :]
                    + pltpu.roll(left, 1, 1) + pltpu.roll(right, 127, 1)
                )
                if n == 3:
                    th = jnp.tanh(us[3][v, t, rows, :])
                    d = 1.0 - th * th
                else:
                    d = ds[n][v, t, rows, :]
                pulled = cf[v][0] * cur[0]
                for w in range(1, V):
                    pulled = pulled + cf[v][w] * cur[w]
                new = a * cur[v] + lap - d * pulled
                if t == 3 and back is not None:
                    f = pltpu.roll(back[rows, :], 127 - (15 + n * V + v), 1)
                    new = new + jnp.where(lane == 127, f, 0.0)
                if n > 0:
                    ls[m + 1][v, t, rows, :] = new
                    ss[m + 1][v, t, rows, :] = kap[t, rows, :] * new
                else:
                    out[v, t, pl.ds(pl.multiple_of(r - 16, 8), 8), :] = new
                if t == 0 and hsum is not None:
                    p = cur[v] * us[n][v, t, rows, :]
                    if n == 3:
                        hsum[v, rows, :] = p
                    else:
                        hsum[v, rows, :] = hsum[v, rows, :] + p

    if n > 0:
        over_rows(body, 0, 18, 6 if len(tiles) == 1 else 2)
    else:
        over_rows(body, 1, 16, 4 if len(tiles) == 1 else 2)


def rows_beside(a):
    lane = lane_of(a.shape)
    up = pltpu.roll(jnp.where(lane == 127, pltpu.roll(a, 1, 0), a), 1, 1)
    down = pltpu.roll(jnp.where(lane == 0, pltpu.roll(a, 31, 0), a), 127, 1)
    return up + down


def put_ring(ring, a):
    ring[0:32, :] = a
    ring[32:64, :] = a
    ring[64:72, :] = a[0:8]


def shifted(ring, amount):
    lane = lane_of((32, 128))
    high, low = amount // 128, amount % 128
    first = ring[pl.ds(high, 32), :]
    second = ring[pl.ds(high + 1, 32), :]
    return pltpu.roll(jnp.where(lane < low, second, first), (128 - low) % 128, 1)


def strips(gat, q, coup, su, sd, sl, sk, tap, shift, ring, tring, face, between):
    row = lax.broadcasted_iota(jnp.int32, (32, 128), 0) * 128 + lane_of((32, 128))

    def get(zone, j):
        return gat[zone, pl.ds(j, 32, stride=CHUNK), :]

    def unpack(zone, carry):
        for v in range(V):
            for k in range(KU):
                su[0, zone, v, k] = get(zone, v * KU + KU - 1 - k)
            for k in range(KL):
                sl[0, zone, v, k] = get(zone, OFF_L + v * KL + KL - 1 - k)
        for k in range(KU):
            sk[zone, k] = get(zone, OFF_K + KU - 1 - k)
        for n in range(4):
            d = get(zone, OFF_M + n).astype(jnp.int32) - row
            base = d[0:1, 0:1]
            d = d - base
            d = jnp.where(d > 2048, d - 4096, d)
            d = jnp.where(d > 2048, d - 4096, d)
            d = jnp.where(d < -2048, d + 4096, d)
            d = jnp.where(d < -2048, d + 4096, d)
            least = jnp.min(d)
            e = d - least
            w = get(zone, OFF_W + n)
            shift[zone, n] = (base[0, 0] + least + 8192) % 4096
            for j in range(6):
                tap[zone, n, j] = jnp.where(e == j, w, 0.0) + jnp.where(e == j - 1, 1.0 - w, 0.0)
        return carry

    lax.fori_loop(0, 2, unpack, 0)

    for n in range(3):
        def faces(zone, carry):
            for v in range(V):
                put_ring(ring.at[zone, v], su[n, zone, v, 0])
            return carry

        lax.fori_loop(0, 2, faces, 0)

        def step(zone, carry):
            ghost = [jnp.zeros((32, 128), F32)] * V
            t = shift[zone, n]
            for j in range(6):
                cj = tap[zone, n, j]
                for v in range(V):
                    ghost[v] = ghost[v] + cj * shifted(ring.at[1 - zone, v], (t + j) % 4096)
            for v in range(V):
                face[zone, n * V + v] = ghost[v]
            for k in range(KU - 1 - n):
                cur = [su[n, zone, v, k] for v in range(V)]
                th = [jnp.tanh(a) for a in cur]
                kk = sk[zone, k]
                for v in range(V):
                    outward = ghost[v] if k == 0 else su[n, zone, v, k - 1]
                    lap = rows_beside(cur[v]) + outward + su[n, zone, v, k + 1] - 4.0 * cur[v]
                    react = coup[v, 0] * th[0]
                    for w in range(1, V):
                        react = react + coup[v, w] * th[w]
                    su[n + 1, zone, v, k] = cur[v] + kk * lap - react
                    if k < n:
                        sd[n, zone, v, k] = 1.0 - th[v] * th[v]
            return carry

        lax.fori_loop(0, 2, step, 0)
        between(n)

    for n in (3, 2, 1, 0):
        m = 3 - n

        def taps(zone, carry):
            for v in range(V):
                put_ring(ring.at[zone, v], sk[zone, 0] * sl[m, zone, v, 0])
            return carry

        lax.fori_loop(0, 2, taps, 0)

        def back(zone, carry):
            other = 1 - zone
            acc = [jnp.zeros((32, 128), F32)] * V
            t = shift[other, n]
            for j in range(6):
                put_ring(tring, tap[other, n, j])
                amount = (8192 - t - j) % 4096
                cj = shifted(tring, amount)
                for v in range(V):
                    acc[v] = acc[v] + cj * shifted(ring.at[other, v], amount)
            for v in range(V):
                face[zone, 15 + n * V + v] = acc[v]
            for k in range(n):
                cur = [sl[m, zone, v, k] for v in range(V)]
                kk = sk[zone, k]
                for v in range(V):
                    s = kk * cur[v]
                    lap = rows_beside(s) + sk[zone, k + 1] * sl[m, zone, v, k + 1] - 4.0 * s
                    if k == 0:
                        lap = lap + acc[v]
                    else:
                        lap = lap + sk[zone, k - 1] * sl[m, zone, v, k - 1]
                    if n == 3:
                        th = jnp.tanh(su[3, zone, v, k])
                        d = 1.0 - th * th
                    else:
                        d = sd[n, zone, v, k]
                    pulled = coup[0, v] * cur[0]
                    for w in range(1, V):
                        pulled = pulled + coup[w, v] * cur[w]
                    sl[m + 1, zone, v, k] = cur[v] + lap - d * pulled
            return carry

        if n > 0:
            lax.fori_loop(0, 2, back, 0)
        else:
            back(q, 0)


def face_columns(face, q, b, cols):
    pad = jnp.zeros((128 - 35, 128), F32)
    for part, dst, size, lo in (((b + 31) % 32, 8, 8, 120), (b, 16, 128, 0), ((b + 1) % 32, 144, 8, 0)):
        rows = face[q, pl.ds(part, 35, stride=32), :]
        cols[dst : dst + size, :] = jnp.concatenate([rows, pad], axis=0).T[lo : lo + size, :]


def scatter_points(hsum, l1, u0, area, proj, ids, dist, partial):
    lane = lane_of((128, 128))
    hs = [hsum[v, 16:144, :] + l1[v, 0, 16:144, :] * u0[v, 0, 16:144, :] for v in range(V)]
    acc = jnp.zeros((128, 128), F32)
    for c in range(3):
        col = proj[c, 0] * hs[0]
        for v in range(1, V):
            col = col + proj[c, v] * hs[v]
        acc = acc + jnp.where(lane == c, pltpu.roll(col, c, 1), 0.0)
    spread = (
        lax.broadcasted_iota(jnp.int32, (128, 384), 1) // 3 == lax.broadcasted_iota(jnp.int32, (128, 384), 0)
    ).astype(F32)
    sens = lax.dot_general(
        acc, spread, (((0,), (0,)), ((), ())), precision=lax.Precision.HIGHEST, preferred_element_type=F32
    )
    sens = [sens[c : c + 1, :] * area[...] for c in range(3)]
    sub_a = lax.broadcasted_iota(jnp.int32, (128, 128), 0)
    sub_b = lax.broadcasted_iota(jnp.int32, (256, 128), 0)
    total = jnp.zeros((384, 256), F32)
    for k in range(8):
        dk = dist[k : k + 1, :]
        om = 1.0 - dk
        om = om * om
        phi = om * om * (4.0 * dk + 1.0)
        idk = ids[k : k + 1, :]
        for wt in range(3):
            cut = slice(wt * 128, (wt + 1) * 128)
            idt = idk[:, cut]
            ch = idt // 256
            rowid = (ch % 2) * 64 + ((ch // 8) % 4) * 16 + ((ch // 2) % 4) * 4 + ch // 32
            mask = sub_a == rowid
            high, low = [], []
            for c in range(3):
                val = phi[:, cut] * sens[c][:, cut]
                hi = val.astype(jnp.bfloat16).astype(F32)
                high.append(jnp.where(mask, hi, 0.0).astype(jnp.bfloat16))
                low.append(jnp.where(mask, val - hi, 0.0).astype(jnp.bfloat16))
            left = jnp.concatenate([jnp.concatenate(high, axis=0), jnp.concatenate(low, axis=0)], axis=1)
            onehot = jnp.where(sub_b == idt % 256, 1.0, 0.0).astype(jnp.bfloat16)
            right = jnp.concatenate([onehot, onehot], axis=1)
            total = total + lax.dot_general(
                left, right, (((1,), (1,)), ((), ())), preferred_element_type=F32
            )
    for c in range(3):
        partial[c] = total[c * 128 : (c + 1) * 128, :]


def window_kernel(
    coup, proj, u_hbm, k_hbm, l_hbm, m_hbm, w_hbm, area, ids, dist, out_hbm, points,
    u0, u1, u2, u3, d0, d1, d2, l4, l3, l2, l1, s4, s3, s2, s1, kap, kc, hsum, outv,
    su, sd, sl, sk, tap, ring, tring, face, cols, shift,
    gat, hu, hl, hk, chunk, mt, wt, partial, r1, q1, r2, q2, r3, q3, r4,
    sem, osem, halo_s, halo_r, first_s, first_r, ph_s, ph_r, core_s, core_r, rs_s, rs_r,
):
    y, b, x, z, c = place()
    q = y % 2
    yp = y + 1 - 2 * q
    b0 = b - c
    twin = b0 + 1 - c
    nxt, prv = (b + 1) % 32, (b + 31) % 32
    us, ds, ls, ss = (u0, u1, u2, u3), (d0, d1, d2), (l4, l3, l2, l1), (s4, s3, s2, s1)

    def loads_of(t):
        cut = pl.ds(t * 128, 128)
        own = pl.ds(16, 128)
        return [
            pltpu.make_async_copy(u_hbm.at[:, 0, :, cut], u0.at[:, t, own, :], sem.at[3 * t]),
            pltpu.make_async_copy(l_hbm.at[:, 0, :, cut], l4.at[:, t, own, :], sem.at[3 * t + 1]),
            pltpu.make_async_copy(k_hbm.at[0, :, cut], kap.at[t, own, :], sem.at[3 * t + 2]),
        ]

    mine = pl.ds(pl.multiple_of(b * 128, 128), 128)
    maps = [
        pltpu.make_async_copy(m_hbm.at[:, 0, mine], mt, sem.at[12]),
        pltpu.make_async_copy(w_hbm.at[:, 0, mine], wt, sem.at[13]),
    ]
    loads = [loads_of(t) for t in range(4)]
    for copy in loads[3] + maps + loads[0] + loads[1] + loads[2]:
        copy.start()

    barrier = pltpu.get_barrier_semaphore()
    peers = [(y, nxt), (y, prv), (yp, b0), (yp, b0 + 1), (y, twin)]
    for d in (1, 2, 3):
        peers.append((y, block_of((x + d) % 4, z, c)))
        peers.append((y, block_of(x, (z + d) % 4, c)))
        peers.append(((y + d) % 4, b))
    for peer in peers:
        pl.semaphore_signal(barrier, inc=1, device_id=peer, device_id_type=MESH)

    halo = []
    for n, (src, dst) in enumerate(((u_hbm, hu), (l_hbm, hl), (k_hbm, hk))):

        def rows(r):
            return src.at[:, 0, pl.ds(r, 8), :] if len(src.shape) == 4 else src.at[0, pl.ds(r, 8), :]

        halo.append(remote(rows(120), dst.at[0], halo_s.at[n], halo_r.at[n], y, nxt))
        halo.append(remote(rows(0), dst.at[1], halo_s.at[3 + n], halo_r.at[3 + n], y, prv))

    for copy in loads[3] + maps:
        copy.wait()
    for v in range(V):
        chunk[KU * v : KU * (v + 1), :] = u0[v, 3, 16:144, :].T[128 - KU :, :]
        chunk[OFF_L + KL * v : OFF_L + KL * (v + 1), :] = l4[v, 3, 16:144, :].T[128 - KL :, :]
    chunk[OFF_K : OFF_K + KU, :] = kap[3, 16:144, :].T[128 - KU :, :]
    chunk[OFF_M : OFF_M + 4, :] = mt[...].astype(F32)
    chunk[OFF_W : OFF_W + 4, :] = wt[...]

    for copy in loads[0] + loads[1] + loads[2]:
        copy.wait()

    def scale(i):
        rows = pl.ds(pl.multiple_of(8 + i * 8, 8), 8)
        for t in range(4):
            k = kap[t, rows, :]
            kc[t, rows, :] = 1.0 - 4.0 * k
            for v in range(V):
                s4[v, t, rows, :] = k * l4[v, t, rows, :]

    every = (0, 1, 2, 3)
    over_rows(scale, 1, 16, 2)
    main_forward(0, us, ds, kap, kc, coup, every, None, inner(2))
    pl.semaphore_wait(barrier, len(peers))

    here = gat.at[q, x, z * 2 + c]
    across = remote(chunk, here, first_s.at[0], first_r.at[c], yp, b0 + q)
    across.start()
    for copy in halo:
        copy.start()

    @pl.when(c == q)
    def _():
        gat[q, x, z * 2 + c] = chunk[...]

    @pl.when(c != q)
    def _():
        remote(chunk, here, first_s.at[1], first_r.at[2], y, b0 + q).start()

    def part(core, stage, d):
        if core == 0:
            if stage == 0:
                return gat.at[0, (x + d) % 4, pl.ds(z * 2, 2)]
            return gat.at[0, :, pl.ds((z + d) % 4 * 2, 2)]
        if stage == 0:
            return gat.at[1, x, pl.ds((z + d) % 4 * 2, 2)]
        return gat.at[1, (x + d) % 4]

    def hops(core, stage):
        copies = []
        for d in (1, 2, 3):
            to = block_of((x + d) % 4, z, c) if core == stage else block_of(x, (z + d) % 4, c)
            n = 3 * stage + d - 1
            copies.append(remote(part(core, stage, 0), part(core, stage, 0), ph_s.at[n], ph_r.at[n], y, to))
        return copies

    def swaps(core, whose):
        return [
            remote(part(whose, 1, d), part(whose, 1, d), core_s.at[d], core_r.at[d], y, twin) for d in range(4)
        ]

    def on_core(core, action):
        @pl.when(c == core)
        def _():
            action(core)

    def first_stage(core):
        @pl.when(q == core)
        def _():
            remote(chunk, here, first_s.at[1], first_r.at[2], y, b0 + q).wait_recv()

        @pl.when(q != core)
        def _():
            for j in range(2):
                remote(chunk, here, first_s.at[0], first_r.at[j], yp, b0 + q).wait_recv()

        for copy in hops(core, 0):
            copy.start()

    def second_stage(core):
        for copy in hops(core, 0):
            copy.wait()
        for copy in hops(core, 1):
            copy.start()
        swaps(core, core)[0].start()

    def third_stage(core):
        copies, sends = hops(core, 1), swaps(core, core)
        for copy in copies:
            copy.wait()
        for copy in sends[1:]:
            copy.start()

    def last_stage(core):
        for copy in swaps(core, core):
            copy.wait_send()
        for copy in swaps(core, 1 - core):
            copy.wait_recv()

    main_forward(1, us, ds, kap, kc, coup, every, None, inner(3))
    for core in range(2):
        on_core(core, first_stage)
    main_forward(2, us, ds, kap, kc, coup, every, None, inner(4))

    for copy in halo:
        copy.wait()
    for t in range(4):
        cut = slice(t * 128, (t + 1) * 128)
        for side, r in ((0, 8), (1, 144)):
            kap[t, r : r + 8, :] = hk[side, :, cut]
            for v in range(V):
                u0[v, t, r : r + 8, :] = hu[side, v, :, cut]
                l4[v, t, r : r + 8, :] = hl[side, v, :, cut]

    over_edges(scale, 1)
    for n in range(3):
        main_forward(n, us, ds, kap, kc, coup, every, None, edges(n + 2))
    for core in range(2):
        on_core(core, second_stage)

    for n in (3, 2, 1):
        main_adjoint(n, us, ds, ls, ss, kap, kc, coup, (0,), None, hsum, outv)
    scatter_points(hsum, l1, u0, area, proj, ids, dist, partial)
    first = remote(
        partial.at[:, pl.ds(pl.multiple_of((1 - c) * 64, 64), 64), :], r1, rs_s.at[0], rs_r.at[0], y, twin
    )
    first.start()

    def sent(slots, got, base, to_of):
        copies = []
        for d in (1, 2, 3):
            index, ty, tb = to_of(d)
            copies.append(
                remote(slots.at[index], got.at[d - 1], rs_s.at[base + d], rs_r.at[base + d], ty, tb)
            )
        return copies

    by_x = sent(q1, r2, 0, lambda d: ((x + d) % 4, y, block_of((x + d) % 4, z, c)))
    by_z = sent(q2, r3, 3, lambda d: ((z + d) % 4, y, block_of(x, (z + d) % 4, c)))
    by_y = sent(q3, r4, 6, lambda d: ((y + d) % 4, (y + d) % 4, b))

    def reduce_stage(step):
        if step == 0:
            first.wait()
            own = pl.multiple_of(c * 64, 64)
            for j in range(4):
                q1[j] = partial[:, pl.ds(own + j * 16, 16), :] + r1[:, j * 16 : (j + 1) * 16, :]
            for copy in by_x:
                copy.start()
        if step == 1:
            for copy in by_x:
                copy.wait()
            total = q1[x] + r2[0] + r2[1] + r2[2]
            for j in range(4):
                q2[j] = total[:, j * 4 : (j + 1) * 4, :]
            for copy in by_z:
                copy.start()
        if step == 2:
            for copy in by_z:
                copy.wait()
            total = q2[z] + r3[0] + r3[1] + r3[2]
            for j in range(4):
                q3[j] = total[:, j, :]
            for copy in by_y:
                copy.start()
        if step == 3:
            for copy in by_y:
                copy.wait()
            points[...] = q3[y] + r4[0] + r4[1] + r4[2]

    for n in (3, 2, 1, 0):
        main_adjoint(n, us, ds, ls, ss, kap, kc, coup, every, None, None, outv)
        if n == 2:
            reduce_stage(0)
            for core in range(2):
                on_core(core, third_stage)
    for core in range(2):
        on_core(core, last_stage)
    across.wait_send()

    @pl.when(c != q)
    def _():
        remote(chunk, here, first_s.at[1], first_r.at[2], y, b0 + q).wait_send()

    reduce_stage(1)

    def between(n):
        if n == 1:
            reduce_stage(2)

    strips(gat.reshape(2, 32 * CHUNK, 128), q, coup, su, sd, sl, sk, tap, shift, ring, tring, face, between)
    reduce_stage(3)
    face_columns(face.reshape(2, 35 * 32, 128), q, b, cols)
    stores = [
        pltpu.make_async_copy(outv.at[:, t], out_hbm.at[:, 0, :, pl.ds(t * 128, 128)], osem.at[t])
        for t in range(4)
    ]
    for copy in stores[:3]:
        copy.start()
    for n in range(3):
        main_forward(n, us, ds, kap, kc, coup, (3,), cols, all_rows)
    for n in (3, 2, 1, 0):
        main_adjoint(n, us, ds, ls, ss, kap, kc, coup, (3,), cols, None, outv)
    stores[3].start()
    for copy in stores:
        copy.wait()


def local(
    start_state, diffusivity, donor_map, donor_weight, coupling, final_cotangent,
    wall_area, wall_projection, center_ids, center_dist,
):
    any_ = pl.BlockSpec(memory_space=pl.ANY)
    vmem = pl.BlockSpec(memory_space=pltpu.VMEM)
    smem = pl.BlockSpec(memory_space=pltpu.SMEM)
    dma = pltpu.SemaphoreType.DMA

    def buf(*shape, dtype=F32):
        return pltpu.VMEM(shape, dtype)

    return pl.pallas_call(
        window_kernel,
        out_shape=(jax.ShapeDtypeStruct((V, 1, 128, 512), F32), jax.ShapeDtypeStruct((3, 256), F32)),
        in_specs=[smem, smem, any_, any_, any_, any_, any_, vmem, vmem, vmem],
        out_specs=(any_, vmem),
        scratch_shapes=[buf(V, 4, ROWS, 128)] * 15
        + [
            buf(4, ROWS, 128),
            buf(4, ROWS, 128),
            buf(V, ROWS, 128),
            buf(V, 4, 128, 128),
            buf(4, 2, V, KU, 32, 128),
            buf(3, 2, V, 2, 32, 128),
            buf(4, 2, V, KL, 32, 128),
            buf(2, KU, 32, 128),
            buf(2, 4, 6, 32, 128),
            buf(2, V, 72, 128),
            buf(72, 128),
            buf(2, 35, 32, 128),
            buf(ROWS, 128),
            pltpu.SMEM((2, 4), jnp.int32),
            buf(2, 4, 8, CHUNK, 128),
            buf(2, V, 8, 512),
            buf(2, V, 8, 512),
            buf(2, 8, 512),
            buf(CHUNK, 128),
            buf(4, 128, dtype=jnp.int32),
            buf(4, 128),
            buf(3, 128, 256),
            buf(3, 64, 256),
            buf(4, 3, 16, 256),
            buf(3, 3, 16, 256),
            buf(4, 3, 4, 256),
            buf(3, 3, 4, 256),
            buf(4, 3, 256),
            buf(3, 3, 256),
        ]
        + [dma((n,)) for n in (14, 4, 6, 6, 2, 3, 6, 6, 4, 4, 10, 10)],
        compiler_params=pltpu.CompilerParams(
            collective_id=0, has_side_effects=True, vmem_limit_bytes=60 * 1024 * 1024
        ),
        name="window",
    )(
        coupling, wall_projection, start_state, diffusivity, final_cotangent, donor_map, donor_weight,
        wall_area, center_ids[0], center_dist[0],
    )


def solution(mesh):
    return jax.shard_map(
        local,
        mesh=mesh,
        in_specs=(
            P(None, "zone", "block", None),
            P("zone", "block", None),
            P(None, "zone", None),
            P(None, "zone", None),
            P(),
            P(None, "zone", "block", None),
            P("zone", "block"),
            P(),
            P("zone", None, "block"),
            P("zone", None, "block"),
        ),
        out_specs=(P(None, "zone", "block", None), P(None, ("zone", "block"))),
        check_vma=False,
    )
```

```python
import functools

import jax
import jax.numpy as jnp
from jax import lax
from jax.experimental import pallas as pl
from jax.experimental.pallas import tpu as pltpu
from jax.sharding import PartitionSpec as P

MESH = pl.DeviceIdType.MESH
F32 = jnp.float32
V = 5
KU = 6
KL = 4
OFF_L = V * KU
OFF_K = OFF_L + V * KL
OFF_M = OFF_K + KU
OFF_W = OFF_M + 4
CHUNK = 64
ROWS = 160


def lane_of(shape):
    return lax.broadcasted_iota(jnp.int32, shape, len(shape) - 1)


def place():
    y = lax.axis_index("zone")
    b = lax.axis_index("block")
    return y, b, b // 8, (b // 2) % 4, b % 2


def block_of(x, z, c):
    return x * 8 + z * 2 + c


def remote(src, dst, send, recv, y, b):
    return pltpu.make_async_remote_copy(
        src_ref=src, dst_ref=dst, send_sem=send, recv_sem=recv, device_id=(y, b), device_id_type=MESH
    )


def over_rows(body, first, count, unroll):
    def several(i, carry):
        for j in range(unroll):
            body(first + i * unroll + j)
        return carry

    lax.fori_loop(0, count // unroll, several, 0)


def over_edges(body, count):
    def side(i, carry):
        for j in range(count):
            body(i * (18 - count) + j)
        return carry

    lax.fori_loop(0, 2, side, 0)


def main_forward(n, us, ds, kap, kc, coup, tiles, ghost, where):
    lane = lane_of((8, 128))
    cf = [[coup[v, w] for w in range(V)] for v in range(V)]
    src, dst, dd = us[n], us[n + 1], ds[n]

    def body(i):
        r = pl.multiple_of(8 + i * 8, 8)
        rows = pl.ds(r, 8)
        for t in tiles:
            k = kap[t, rows, :]
            a = kc[t, rows, :]
            cur = [src[v, t, rows, :] for v in range(V)]
            th = [jnp.tanh(e) for e in cur]
            for v in range(V):
                if t == 0:
                    left = jnp.where(lane == 127, 0.0, cur[v])
                else:
                    left = jnp.where(lane == 127, src[v, t - 1, rows, :], cur[v])
                if t < 3:
                    right = jnp.where(lane == 0, src[v, t + 1, rows, :], cur[v])
                elif ghost is None:
                    right = jnp.where(lane == 0, 0.0, cur[v])
                else:
                    g = pltpu.roll(ghost[rows, :], (128 - (n * V + v)) % 128, 1)
                    right = jnp.where(lane == 0, g, cur[v])
                lap = (
                    src[v, t, pl.ds(r - 1, 8), :] + src[v, t, pl.ds(r + 1, 8), :]
                    + pltpu.roll(left, 1, 1) + pltpu.roll(right, 127, 1)
                )
                react = cf[v][0] * th[0]
                for w in range(1, V):
                    react = react + cf[v][w] * th[w]
                dst[v, t, rows, :] = a * cur[v] + k * lap - react
                dd[v, t, rows, :] = 1.0 - th[v] * th[v]

    where(body)


def inner(margin):
    return lambda body: over_rows(body, margin, 18 - 2 * margin, 2)


def edges(count):
    return lambda body: over_edges(body, count)


def all_rows(body):
    over_rows(body, 0, 18, 6)


def main_adjoint(n, us, ds, ls, ss, kap, kc, coup, tiles, back, hsum, out, where=None):
    lane = lane_of((8, 128))
    cf = [[coup[w, v] for w in range(V)] for v in range(V)]
    m = 3 - n
    lam, sca = ls[m], ss[m]

    def body(i):
        r = pl.multiple_of(8 + i * 8, 8)
        rows = pl.ds(r, 8)
        for t in tiles:
            cur = [lam[v, t, rows, :] for v in range(V)]
            a = kc[t, rows, :]
            for v in range(V):
                s = sca[v, t, rows, :]
                if t == 0:
                    left = jnp.where(lane == 127, 0.0, s)
                else:
                    left = jnp.where(lane == 127, sca[v, t - 1, rows, :], s)
                right = jnp.where(lane == 0, sca[v, t + 1, rows, :] if t < 3 else 0.0, s)
                lap = (
                    sca[v, t, pl.ds(r - 1, 8), :] + sca[v, t, pl.ds(r + 1, 8), :]
                    + pltpu.roll(left, 1, 1) + pltpu.roll(right, 127, 1)
                )
                if n == 3:
                    th = jnp.tanh(us[3][v, t, rows, :])
                    d = 1.0 - th * th
                else:
                    d = ds[n][v, t, rows, :]
                pulled = cf[v][0] * cur[0]
                for w in range(1, V):
                    pulled = pulled + cf[v][w] * cur[w]
                new = a * cur[v] + lap - d * pulled
                if t == 3 and back is not None:
                    f = pltpu.roll(back[rows, :], 127 - (15 + n * V + v), 1)
                    new = new + jnp.where(lane == 127, f, 0.0)
                if n > 0:
                    ls[m + 1][v, t, rows, :] = new
                    ss[m + 1][v, t, rows, :] = kap[t, rows, :] * new
                else:
                    out[v, t, pl.ds(pl.multiple_of(r - 16, 8), 8), :] = new
                if t == 0 and hsum is not None:
                    p = cur[v] * us[n][v, t, rows, :]
                    if n == 3:
                        hsum[v, rows, :] = p
                    else:
                        hsum[v, rows, :] = hsum[v, rows, :] + p

    if where is not None:
        where(body)
    elif n > 0:
        over_rows(body, 0, 18, 6 if len(tiles) == 1 else 2)
    else:
        over_rows(body, 1, 16, 4 if len(tiles) == 1 else 2)


def rows_beside(a):
    lane = lane_of(a.shape)
    up = pltpu.roll(jnp.where(lane == 127, pltpu.roll(a, 1, 0), a), 1, 1)
    down = pltpu.roll(jnp.where(lane == 0, pltpu.roll(a, 31, 0), a), 127, 1)
    return up + down


def put_ring(ring, a):
    ring[0:32, :] = a
    ring[32:64, :] = a
    ring[64:72, :] = a[0:8]


def shifted(ring, amount):
    lane = lane_of((32, 128))
    high, low = amount // 128, amount % 128
    first = ring[pl.ds(high, 32), :]
    second = ring[pl.ds(high + 1, 32), :]
    return pltpu.roll(jnp.where(lane < low, second, first), (128 - low) % 128, 1)


def strips(gat, q, coup, su, sd, sl, sk, tap, shift, ring, tring, face, turned, between):
    row = lax.broadcasted_iota(jnp.int32, (32, 128), 0) * 128 + lane_of((32, 128))

    def get(zone, j):
        return turned[j]

    def unpack(zone, carry):
        for j in range(CHUNK // 8):
            for i in range(4):
                turned[j * 8 : (j + 1) * 8, i * 8 : (i + 1) * 8, :] = jnp.swapaxes(
                    gat[zone, i, :, j * 8 : (j + 1) * 8, :], 0, 1
                )
        for v in range(V):
            for k in range(KU):
                su[0, zone, v, k] = get(zone, v * KU + KU - 1 - k)
            for k in range(KL):
                sl[0, zone, v, k] = get(zone, OFF_L + v * KL + KL - 1 - k)
        for k in range(KU):
            sk[zone, k] = get(zone, OFF_K + KU - 1 - k)
        for n in range(4):
            d = get(zone, OFF_M + n).astype(jnp.int32) - row
            base = d[0:1, 0:1]
            d = d - base
            d = jnp.where(d > 2048, d - 4096, d)
            d = jnp.where(d > 2048, d - 4096, d)
            d = jnp.where(d < -2048, d + 4096, d)
            d = jnp.where(d < -2048, d + 4096, d)
            least = jnp.min(d)
            e = d - least
            w = get(zone, OFF_W + n)
            shift[zone, n] = (base[0, 0] + least + 8192) % 4096
            for j in range(6):
                tap[zone, n, j] = jnp.where(e == j, w, 0.0) + jnp.where(e == j - 1, 1.0 - w, 0.0)
        return carry

    lax.fori_loop(0, 2, unpack, 0)

    for n in range(3):
        def faces(zone, carry):
            for v in range(V):
                put_ring(ring.at[zone, v], su[n, zone, v, 0])
            return carry

        lax.fori_loop(0, 2, faces, 0)

        def step(zone, carry):
            ghost = [jnp.zeros((32, 128), F32)] * V
            t = shift[zone, n]
            for j in range(6):
                cj = tap[zone, n, j]
                for v in range(V):
                    ghost[v] = ghost[v] + cj * shifted(ring.at[1 - zone, v], (t + j) % 4096)
            for v in range(V):
                face[zone, n * V + v] = ghost[v]
            for k in range(KU - 1 - n):
                cur = [su[n, zone, v, k] for v in range(V)]
                th = [jnp.tanh(a) for a in cur]
                kk = sk[zone, k]
                for v in range(V):
                    outward = ghost[v] if k == 0 else su[n, zone, v, k - 1]
                    lap = rows_beside(cur[v]) + outward + su[n, zone, v, k + 1] - 4.0 * cur[v]
                    react = coup[v, 0] * th[0]
                    for w in range(1, V):
                        react = react + coup[v, w] * th[w]
                    su[n + 1, zone, v, k] = cur[v] + kk * lap - react
                    if k < n:
                        sd[n, zone, v, k] = 1.0 - th[v] * th[v]
            return carry

        lax.fori_loop(0, 2, step, 0)
        between(n)

    for n in (3, 2, 1, 0):
        m = 3 - n

        def taps(zone, carry):
            for v in range(V):
                put_ring(ring.at[zone, v], sk[zone, 0] * sl[m, zone, v, 0])
            return carry

        lax.fori_loop(0, 2, taps, 0)

        def back(zone, carry):
            other = 1 - zone
            acc = [jnp.zeros((32, 128), F32)] * V
            t = shift[other, n]
            for j in range(6):
                put_ring(tring, tap[other, n, j])
                amount = (8192 - t - j) % 4096
                cj = shifted(tring, amount)
                for v in range(V):
                    acc[v] = acc[v] + cj * shifted(ring.at[other, v], amount)
            for v in range(V):
                face[zone, 15 + n * V + v] = acc[v]
            for k in range(n):
                cur = [sl[m, zone, v, k] for v in range(V)]
                kk = sk[zone, k]
                for v in range(V):
                    s = kk * cur[v]
                    lap = rows_beside(s) + sk[zone, k + 1] * sl[m, zone, v, k + 1] - 4.0 * s
                    if k == 0:
                        lap = lap + acc[v]
                    else:
                        lap = lap + sk[zone, k - 1] * sl[m, zone, v, k - 1]
                    if n == 3:
                        th = jnp.tanh(su[3, zone, v, k])
                        d = 1.0 - th * th
                    else:
                        d = sd[n, zone, v, k]
                    pulled = coup[0, v] * cur[0]
                    for w in range(1, V):
                        pulled = pulled + coup[w, v] * cur[w]
                    sl[m + 1, zone, v, k] = cur[v] + lap - d * pulled
            return carry

        if n > 0:
            lax.fori_loop(0, 2, back, 0)
        else:
            back(q, 0)


def face_columns(face, q, b, cols):
    pad = jnp.zeros((128 - 35, 128), F32)
    for part, dst, size, lo in (((b + 31) % 32, 8, 8, 120), (b, 16, 128, 0), ((b + 1) % 32, 144, 8, 0)):
        rows = face[q, pl.ds(part, 35, stride=32), :]
        cols[dst : dst + size, :] = jnp.concatenate([rows, pad], axis=0).T[lo : lo + size, :]


def scatter_points(hsum, l1, u0, area, proj, ids, dist, partial):
    lane = lane_of((128, 128))
    hs = [hsum[v, 16:144, :] + l1[v, 0, 16:144, :] * u0[v, 0, 16:144, :] for v in range(V)]
    acc = jnp.zeros((128, 128), F32)
    for c in range(3):
        col = proj[c, 0] * hs[0]
        for v in range(1, V):
            col = col + proj[c, v] * hs[v]
        acc = acc + jnp.where(lane == c, pltpu.roll(col, c, 1), 0.0)
    spread = (
        lax.broadcasted_iota(jnp.int32, (128, 384), 1) // 3 == lax.broadcasted_iota(jnp.int32, (128, 384), 0)
    ).astype(F32)
    sens = lax.dot_general(
        acc, spread, (((0,), (0,)), ((), ())), precision=lax.Precision.HIGHEST, preferred_element_type=F32
    )
    sens = [sens[c : c + 1, :] * area[...] for c in range(3)]
    sub_a = lax.broadcasted_iota(jnp.int32, (128, 128), 0)
    sub_b = lax.broadcasted_iota(jnp.int32, (256, 128), 0)
    total = jnp.zeros((384, 256), F32)
    for k in range(8):
        dk = dist[k : k + 1, :]
        om = 1.0 - dk
        om = om * om
        phi = om * om * (4.0 * dk + 1.0)
        idk = ids[k : k + 1, :]
        for wt in range(3):
            cut = slice(wt * 128, (wt + 1) * 128)
            idt = idk[:, cut]
            ch = idt // 256
            rowid = (ch % 2) * 64 + ((ch // 8) % 4) * 16 + ((ch // 2) % 4) * 4 + ch // 32
            mask = sub_a == rowid
            high, low = [], []
            for c in range(3):
                val = phi[:, cut] * sens[c][:, cut]
                hi = val.astype(jnp.bfloat16).astype(F32)
                high.append(jnp.where(mask, hi, 0.0).astype(jnp.bfloat16))
                low.append(jnp.where(mask, val - hi, 0.0).astype(jnp.bfloat16))
            left = jnp.concatenate([jnp.concatenate(high, axis=0), jnp.concatenate(low, axis=0)], axis=1)
            onehot = jnp.where(sub_b == idt % 256, 1.0, 0.0).astype(jnp.bfloat16)
            right = jnp.concatenate([onehot, onehot], axis=1)
            total = total + lax.dot_general(
                left, right, (((1,), (1,)), ((), ())), preferred_element_type=F32
            )
    for c in range(3):
        partial[c] = total[c * 128 : (c + 1) * 128, :]


def window_kernel(
    coup, proj, u_hbm, k_hbm, l_hbm, m_hbm, w_hbm, area, ids, dist, out_hbm, points,
    u0, u1, u2, u3, d0, d1, d2, l4, l3, l2, l1, s4, s3, s2, s1, kap, kc, hsum, outv,
    su, sd, sl, sk, tap, ring, tring, face, cols, shift,
    gat, hu, hl, hk, chunk, mt, wt, partial, r1, q1, r2, q2, r3, q3, r4, turned,
    sem, osem, halo_s, halo_r, first_s, first_r, ph_s, ph_r, core_s, core_r, rs_s, rs_r,
):
    y, b, x, z, c = place()
    q = y % 2
    yp = y + 1 - 2 * q
    b0 = b - c
    twin = b0 + 1 - c
    nxt, prv = (b + 1) % 32, (b + 31) % 32
    us, ds, ls, ss = (u0, u1, u2, u3), (d0, d1, d2), (l4, l3, l2, l1), (s4, s3, s2, s1)

    def loads_of(t):
        cut = pl.ds(t * 128, 128)
        own = pl.ds(16, 128)
        return [
            pltpu.make_async_copy(u_hbm.at[:, 0, :, cut], u0.at[:, t, own, :], sem.at[3 * t]),
            pltpu.make_async_copy(l_hbm.at[:, 0, :, cut], l4.at[:, t, own, :], sem.at[3 * t + 1]),
            pltpu.make_async_copy(k_hbm.at[0, :, cut], kap.at[t, own, :], sem.at[3 * t + 2]),
        ]

    mine = pl.ds(pl.multiple_of(b * 128, 128), 128)
    maps = [
        pltpu.make_async_copy(m_hbm.at[:, 0, mine], mt, sem.at[12]),
        pltpu.make_async_copy(w_hbm.at[:, 0, mine], wt, sem.at[13]),
    ]
    loads = [loads_of(t) for t in range(4)]
    for copy in loads[3] + maps + loads[0] + loads[1] + loads[2]:
        copy.start()

    barrier = pltpu.get_barrier_semaphore()
    peers = [(y, nxt), (y, prv), (yp, b0), (yp, b0 + 1), (y, twin)]
    for d in (1, 2, 3):
        peers.append((y, block_of((x + d) % 4, z, c)))
        peers.append((y, block_of(x, (z + d) % 4, c)))
        peers.append(((y + d) % 4, b))
    for peer in peers:
        pl.semaphore_signal(barrier, inc=1, device_id=peer, device_id_type=MESH)

    halo = []
    for n, (src, dst) in enumerate(((u_hbm, hu), (l_hbm, hl), (k_hbm, hk))):

        def rows(r):
            return src.at[:, 0, pl.ds(r, 8), :] if len(src.shape) == 4 else src.at[0, pl.ds(r, 8), :]

        halo.append(remote(rows(120), dst.at[0], halo_s.at[n], halo_r.at[n], y, nxt))
        halo.append(remote(rows(0), dst.at[1], halo_s.at[3 + n], halo_r.at[3 + n], y, prv))

    for copy in loads[3] + maps:
        copy.wait()
    for v in range(V):
        chunk[KU * v : KU * (v + 1), :] = u0[v, 3, 16:144, :].T[128 - KU :, :]
        chunk[OFF_L + KL * v : OFF_L + KL * (v + 1), :] = l4[v, 3, 16:144, :].T[128 - KL :, :]
    chunk[OFF_K : OFF_K + KU, :] = kap[3, 16:144, :].T[128 - KU :, :]
    chunk[OFF_M : OFF_M + 4, :] = mt[...].astype(F32)
    chunk[OFF_W : OFF_W + 4, :] = wt[...]

    for copy in loads[0] + loads[1] + loads[2]:
        copy.wait()

    def scale(i):
        rows = pl.ds(pl.multiple_of(8 + i * 8, 8), 8)
        for t in range(4):
            k = kap[t, rows, :]
            kc[t, rows, :] = 1.0 - 4.0 * k
            for v in range(V):
                s4[v, t, rows, :] = k * l4[v, t, rows, :]

    every = (0, 1, 2, 3)
    over_rows(scale, 1, 16, 2)
    main_forward(0, us, ds, kap, kc, coup, every, None, inner(2))
    pl.semaphore_wait(barrier, len(peers))

    here = gat.at[q, x, z * 2 + c]
    across = remote(chunk, here, first_s.at[0], first_r.at[c], yp, b0 + q)
    across.start()
    for copy in halo:
        copy.start()

    @pl.when(c == q)
    def _():
        gat[q, x, z * 2 + c] = chunk[...]

    @pl.when(c != q)
    def _():
        remote(chunk, here, first_s.at[1], first_r.at[2], y, b0 + q).start()

    def part(core, stage, d):
        if core == 0:
            if stage == 0:
                return gat.at[0, (x + d) % 4, pl.ds(z * 2, 2)]
            return gat.at[0, :, pl.ds((z + d) % 4 * 2, 2)]
        if stage == 0:
            return gat.at[1, x, pl.ds((z + d) % 4 * 2, 2)]
        return gat.at[1, (x + d) % 4]

    def hops(core, stage):
        copies = []
        for d in (1, 2, 3):
            to = block_of((x + d) % 4, z, c) if core == stage else block_of(x, (z + d) % 4, c)
            n = 3 * stage + d - 1
            copies.append(remote(part(core, stage, 0), part(core, stage, 0), ph_s.at[n], ph_r.at[n], y, to))
        return copies

    def swaps(core, whose):
        return [
            remote(part(whose, 1, d), part(whose, 1, d), core_s.at[d], core_r.at[d], y, twin) for d in range(4)
        ]

    def on_core(core, action):
        @pl.when(c == core)
        def _():
            action(core)

    def first_stage(core):
        @pl.when(q == core)
        def _():
            remote(chunk, here, first_s.at[1], first_r.at[2], y, b0 + q).wait_recv()

        @pl.when(q != core)
        def _():
            for j in range(2):
                remote(chunk, here, first_s.at[0], first_r.at[j], yp, b0 + q).wait_recv()

        for copy in hops(core, 0):
            copy.start()

    def second_stage(core):
        for copy in hops(core, 0):
            copy.wait()
        for copy in hops(core, 1):
            copy.start()
        swaps(core, core)[0].start()

    def third_stage(core):
        copies, sends = hops(core, 1), swaps(core, core)
        for copy in copies:
            copy.wait()
        for copy in sends[1:]:
            copy.start()

    def last_stage(core):
        for copy in swaps(core, core):
            copy.wait_send()
        for copy in swaps(core, 1 - core):
            copy.wait_recv()

    main_forward(1, us, ds, kap, kc, coup, every, None, inner(3))
    for core in range(2):
        on_core(core, first_stage)
    main_forward(2, us, ds, kap, kc, coup, every, None, inner(4))

    for n in (3, 2, 1):
        main_adjoint(n, us, ds, ls, ss, kap, kc, coup, every, None, None, outv, inner(8 - n))

    for copy in halo:
        copy.wait()
    for t in range(4):
        cut = slice(t * 128, (t + 1) * 128)
        for side, r in ((0, 8), (1, 144)):
            kap[t, r : r + 8, :] = hk[side, :, cut]
            for v in range(V):
                u0[v, t, r : r + 8, :] = hu[side, v, :, cut]
                l4[v, t, r : r + 8, :] = hl[side, v, :, cut]

    over_edges(scale, 1)
    for n in range(3):
        main_forward(n, us, ds, kap, kc, coup, every, None, edges(n + 2))
    for core in range(2):
        on_core(core, second_stage)

    for n in (3, 2, 1):
        main_adjoint(n, us, ds, ls, ss, kap, kc, coup, (0,), None, hsum, outv)
    scatter_points(hsum, l1, u0, area, proj, ids, dist, partial)
    first = remote(
        partial.at[:, pl.ds(pl.multiple_of((1 - c) * 64, 64), 64), :], r1, rs_s.at[0], rs_r.at[0], y, twin
    )
    first.start()

    def sent(slots, got, base, to_of):
        copies = []
        for d in (1, 2, 3):
            index, ty, tb = to_of(d)
            copies.append(
                remote(slots.at[index], got.at[d - 1], rs_s.at[base + d], rs_r.at[base + d], ty, tb)
            )
        return copies

    by_x = sent(q1, r2, 0, lambda d: ((x + d) % 4, y, block_of((x + d) % 4, z, c)))
    by_z = sent(q2, r3, 3, lambda d: ((z + d) % 4, y, block_of(x, (z + d) % 4, c)))
    by_y = sent(q3, r4, 6, lambda d: ((y + d) % 4, (y + d) % 4, b))

    def reduce_stage(step):
        if step == 0:
            first.wait()
            own = pl.multiple_of(c * 64, 64)
            for j in range(4):
                q1[j] = partial[:, pl.ds(own + j * 16, 16), :] + r1[:, j * 16 : (j + 1) * 16, :]
            for copy in by_x:
                copy.start()
        if step == 1:
            for copy in by_x:
                copy.wait()
            total = q1[x] + r2[0] + r2[1] + r2[2]
            for j in range(4):
                q2[j] = total[:, j * 4 : (j + 1) * 4, :]
            for copy in by_z:
                copy.start()
        if step == 2:
            for copy in by_z:
                copy.wait()
            total = q2[z] + r3[0] + r3[1] + r3[2]
            for j in range(4):
                q3[j] = total[:, j, :]
            for copy in by_y:
                copy.start()
        if step == 3:
            for copy in by_y:
                copy.wait()
            points[...] = q3[y] + r4[0] + r4[1] + r4[2]

    for n in (3, 2, 1, 0):
        rest = None if n == 0 else edges(8 - n)
        main_adjoint(n, us, ds, ls, ss, kap, kc, coup, every, None, None, outv, rest)
        if n == 2:
            reduce_stage(0)
            for core in range(2):
                on_core(core, third_stage)
    for core in range(2):
        on_core(core, last_stage)
    across.wait_send()

    @pl.when(c != q)
    def _():
        remote(chunk, here, first_s.at[1], first_r.at[2], y, b0 + q).wait_send()


    def between(n):
        if n == 0:
            reduce_stage(1)
        if n == 2:
            reduce_stage(2)

    strips(gat, q, coup, su, sd, sl, sk, tap, shift, ring, tring, face, turned, between)
    face_columns(face.reshape(2, 35 * 32, 128), q, b, cols)
    stores = [
        pltpu.make_async_copy(outv.at[:, t], out_hbm.at[:, 0, :, pl.ds(t * 128, 128)], osem.at[t])
        for t in range(4)
    ]
    for copy in stores[:3]:
        copy.start()
    for n in range(3):
        main_forward(n, us, ds, kap, kc, coup, (3,), cols, all_rows)
    for n in (3, 2, 1, 0):
        main_adjoint(n, us, ds, ls, ss, kap, kc, coup, (3,), cols, None, outv)
    stores[3].start()
    reduce_stage(3)
    for copy in stores:
        copy.wait()


def local(
    start_state, diffusivity, donor_map, donor_weight, coupling, final_cotangent,
    wall_area, wall_projection, center_ids, center_dist,
):
    any_ = pl.BlockSpec(memory_space=pl.ANY)
    vmem = pl.BlockSpec(memory_space=pltpu.VMEM)
    smem = pl.BlockSpec(memory_space=pltpu.SMEM)
    dma = pltpu.SemaphoreType.DMA

    def buf(*shape, dtype=F32):
        return pltpu.VMEM(shape, dtype)

    return pl.pallas_call(
        window_kernel,
        out_shape=(jax.ShapeDtypeStruct((V, 1, 128, 512), F32), jax.ShapeDtypeStruct((3, 256), F32)),
        in_specs=[smem, smem, any_, any_, any_, any_, any_, vmem, vmem, vmem],
        out_specs=(any_, vmem),
        scratch_shapes=[buf(V, 4, ROWS, 128)] * 15
        + [
            buf(4, ROWS, 128),
            buf(4, ROWS, 128),
            buf(V, ROWS, 128),
            buf(V, 4, 128, 128),
            buf(4, 2, V, KU, 32, 128),
            buf(3, 2, V, 2, 32, 128),
            buf(4, 2, V, KL, 32, 128),
            buf(2, KU, 32, 128),
            buf(2, 4, 6, 32, 128),
            buf(2, V, 72, 128),
            buf(72, 128),
            buf(2, 35, 32, 128),
            buf(ROWS, 128),
            pltpu.SMEM((2, 4), jnp.int32),
            buf(2, 4, 8, CHUNK, 128),
            buf(2, V, 8, 512),
            buf(2, V, 8, 512),
            buf(2, 8, 512),
            buf(CHUNK, 128),
            buf(4, 128, dtype=jnp.int32),
            buf(4, 128),
            buf(3, 128, 256),
            buf(3, 64, 256),
            buf(4, 3, 16, 256),
            buf(3, 3, 16, 256),
            buf(4, 3, 4, 256),
            buf(3, 3, 4, 256),
            buf(4, 3, 256),
            buf(3, 3, 256),
            buf(CHUNK, 32, 128),
        ]
        + [dma((n,)) for n in (14, 4, 6, 6, 2, 3, 6, 6, 4, 4, 10, 10)],
        compiler_params=pltpu.CompilerParams(
            collective_id=0, has_side_effects=True, vmem_limit_bytes=60 * 1024 * 1024
        ),
        name="window",
    )(
        coupling, wall_projection, start_state, diffusivity, final_cotangent, donor_map, donor_weight,
        wall_area, center_ids[0], center_dist[0],
    )


def solution(mesh):
    return jax.shard_map(
        local,
        mesh=mesh,
        in_specs=(
            P(None, "zone", "block", None),
            P("zone", "block", None),
            P(None, "zone", None),
            P(None, "zone", None),
            P(),
            P(None, "zone", "block", None),
            P("zone", "block"),
            P(),
            P("zone", None, "block"),
            P("zone", None, "block"),
        ),
        out_specs=(P(None, "zone", "block", None), P(None, ("zone", "block"))),
        check_vma=False,
    )
```

```python
import functools

import jax
import jax.numpy as jnp
from jax import lax
from jax.experimental import pallas as pl
from jax.experimental.pallas import tpu as pltpu
from jax.sharding import PartitionSpec as P

MESH = pl.DeviceIdType.MESH
F32 = jnp.float32
V = 5
KU = 6
KL = 4
OFF_L = V * KU
OFF_K = OFF_L + V * KL
OFF_M = OFF_K + KU
OFF_W = OFF_M + 4
CHUNK = 64
ROWS = 160


def lane_of(shape):
    return lax.broadcasted_iota(jnp.int32, shape, len(shape) - 1)


def place():
    y = lax.axis_index("zone")
    b = lax.axis_index("block")
    return y, b, b // 8, (b // 2) % 4, b % 2


def block_of(x, z, c):
    return x * 8 + z * 2 + c


def remote(src, dst, send, recv, y, b):
    return pltpu.make_async_remote_copy(
        src_ref=src, dst_ref=dst, send_sem=send, recv_sem=recv, device_id=(y, b), device_id_type=MESH
    )


def over_rows(body, first, count, unroll):
    def several(i, carry):
        for j in range(unroll):
            body(first + i * unroll + j)
        return carry

    lax.fori_loop(0, count // unroll, several, 0)


def over_edges(body, count):
    def side(i, carry):
        for j in range(count):
            body(i * (18 - count) + j)
        return carry

    lax.fori_loop(0, 2, side, 0)


def main_forward(n, us, ds, kap, kc, coup, tiles, ghost, where):
    lane = lane_of((8, 128))
    cf = [[coup[v, w] for w in range(V)] for v in range(V)]
    src, dst, dd = us[n], us[n + 1], ds[n]

    def body(i):
        r = pl.multiple_of(8 + i * 8, 8)
        rows = pl.ds(r, 8)
        for t in tiles:
            k = kap[t, rows, :]
            a = kc[t, rows, :]
            cur = [src[v, t, rows, :] for v in range(V)]
            th = [jnp.tanh(e) for e in cur]
            for v in range(V):
                if t == 0:
                    left = jnp.where(lane == 127, 0.0, cur[v])
                else:
                    left = jnp.where(lane == 127, src[v, t - 1, rows, :], cur[v])
                if t < 3:
                    right = jnp.where(lane == 0, src[v, t + 1, rows, :], cur[v])
                elif ghost is None:
                    right = jnp.where(lane == 0, 0.0, cur[v])
                else:
                    g = pltpu.roll(ghost[rows, :], (128 - (n * V + v)) % 128, 1)
                    right = jnp.where(lane == 0, g, cur[v])
                lap = (
                    src[v, t, pl.ds(r - 1, 8), :] + src[v, t, pl.ds(r + 1, 8), :]
                    + pltpu.roll(left, 1, 1) + pltpu.roll(right, 127, 1)
                )
                react = cf[v][0] * th[0]
                for w in range(1, V):
                    react = react + cf[v][w] * th[w]
                dst[v, t, rows, :] = a * cur[v] + k * lap - react
                dd[v, t, rows, :] = 1.0 - th[v] * th[v]

    where(body)


def inner(margin):
    return lambda body: over_rows(body, margin, 18 - 2 * margin, 2)


def edges(count):
    return lambda body: over_edges(body, count)


def all_rows(body):
    over_rows(body, 0, 18, 6)


def main_adjoint(n, us, ds, ls, ss, kap, kc, coup, tiles, back, hsum, out, where=None):
    lane = lane_of((8, 128))
    cf = [[coup[w, v] for w in range(V)] for v in range(V)]
    m = 3 - n
    lam, sca = ls[m], ss[m]

    def body(i):
        r = pl.multiple_of(8 + i * 8, 8)
        rows = pl.ds(r, 8)
        for t in tiles:
            cur = [lam[v, t, rows, :] for v in range(V)]
            a = kc[t, rows, :]
            for v in range(V):
                s = sca[v, t, rows, :]
                if t == 0:
                    left = jnp.where(lane == 127, 0.0, s)
                else:
                    left = jnp.where(lane == 127, sca[v, t - 1, rows, :], s)
                right = jnp.where(lane == 0, sca[v, t + 1, rows, :] if t < 3 else 0.0, s)
                lap = (
                    sca[v, t, pl.ds(r - 1, 8), :] + sca[v, t, pl.ds(r + 1, 8), :]
                    + pltpu.roll(left, 1, 1) + pltpu.roll(right, 127, 1)
                )
                if n == 3:
                    th = jnp.tanh(us[3][v, t, rows, :])
                    d = 1.0 - th * th
                else:
                    d = ds[n][v, t, rows, :]
                pulled = cf[v][0] * cur[0]
                for w in range(1, V):
                    pulled = pulled + cf[v][w] * cur[w]
                new = a * cur[v] + lap - d * pulled
                if t == 3 and back is not None:
                    f = pltpu.roll(back[rows, :], 127 - (15 + n * V + v), 1)
                    new = new + jnp.where(lane == 127, f, 0.0)
                if n > 0:
                    ls[m + 1][v, t, rows, :] = new
                    ss[m + 1][v, t, rows, :] = kap[t, rows, :] * new
                else:
                    out[v, t, pl.ds(pl.multiple_of(r - 16, 8), 8), :] = new
                if t == 0 and hsum is not None:
                    p = cur[v] * us[n][v, t, rows, :]
                    if n == 3:
                        hsum[v, rows, :] = p
                    else:
                        hsum[v, rows, :] = hsum[v, rows, :] + p

    if where is not None:
        where(body)
    elif n > 0:
        over_rows(body, 0, 18, 6 if len(tiles) == 1 else 2)
    else:
        over_rows(body, 1, 16, 4 if len(tiles) == 1 else 2)


def rows_beside(a):
    lane = lane_of(a.shape)
    up = pltpu.roll(jnp.where(lane == 127, pltpu.roll(a, 1, 0), a), 1, 1)
    down = pltpu.roll(jnp.where(lane == 0, pltpu.roll(a, 31, 0), a), 127, 1)
    return up + down


def put_ring(ring, a):
    ring[0:32, :] = a
    ring[32:64, :] = a
    ring[64:72, :] = a[0:8]


def shifted(ring, amount):
    lane = lane_of((32, 128))
    high, low = amount // 128, amount % 128
    first = ring[pl.ds(high, 32), :]
    second = ring[pl.ds(high + 1, 32), :]
    return pltpu.roll(jnp.where(lane < low, second, first), (128 - low) % 128, 1)


def strips(gat, q, coup, su, sd, sl, sk, tap, shift, ring, tring, face, turned, between):
    row = lax.broadcasted_iota(jnp.int32, (32, 128), 0) * 128 + lane_of((32, 128))

    def get(zone, j):
        return turned[j]

    def unpack(zone, carry):
        for j in range(CHUNK // 8):
            for i in range(4):
                turned[j * 8 : (j + 1) * 8, i * 8 : (i + 1) * 8, :] = jnp.swapaxes(
                    gat[zone, i, :, j * 8 : (j + 1) * 8, :], 0, 1
                )
        for v in range(V):
            for k in range(KU):
                su[0, zone, v, k] = get(zone, v * KU + KU - 1 - k)
            for k in range(KL):
                sl[0, zone, v, k] = get(zone, OFF_L + v * KL + KL - 1 - k)
        for k in range(KU):
            sk[zone, k] = get(zone, OFF_K + KU - 1 - k)
        for n in range(4):
            d = get(zone, OFF_M + n).astype(jnp.int32) - row
            base = d[0:1, 0:1]
            d = d - base
            d = jnp.where(d > 2048, d - 4096, d)
            d = jnp.where(d > 2048, d - 4096, d)
            d = jnp.where(d < -2048, d + 4096, d)
            d = jnp.where(d < -2048, d + 4096, d)
            least = jnp.min(d)
            e = d - least
            w = get(zone, OFF_W + n)
            shift[zone, n] = (base[0, 0] + least + 8192) % 4096
            for j in range(6):
                tap[zone, n, j] = jnp.where(e == j, w, 0.0) + jnp.where(e == j - 1, 1.0 - w, 0.0)
        return carry

    lax.fori_loop(0, 2, unpack, 0)

    for n in range(3):
        def faces(zone, carry):
            for v in range(V):
                put_ring(ring.at[zone, v], su[n, zone, v, 0])
            return carry

        lax.fori_loop(0, 2, faces, 0)

        def step(zone, carry):
            ghost = [jnp.zeros((32, 128), F32)] * V
            t = shift[zone, n]
            for j in range(6):
                cj = tap[zone, n, j]
                for v in range(V):
                    ghost[v] = ghost[v] + cj * shifted(ring.at[1 - zone, v], (t + j) % 4096)
            for v in range(V):
                face[zone, n * V + v] = ghost[v]
            for k in range(KU - 1 - n):
                cur = [su[n, zone, v, k] for v in range(V)]
                th = [jnp.tanh(a) for a in cur]
                kk = sk[zone, k]
                for v in range(V):
                    outward = ghost[v] if k == 0 else su[n, zone, v, k - 1]
                    lap = rows_beside(cur[v]) + outward + su[n, zone, v, k + 1] - 4.0 * cur[v]
                    react = coup[v, 0] * th[0]
                    for w in range(1, V):
                        react = react + coup[v, w] * th[w]
                    su[n + 1, zone, v, k] = cur[v] + kk * lap - react
                    if k < n:
                        sd[n, zone, v, k] = 1.0 - th[v] * th[v]
            return carry

        lax.fori_loop(0, 2, step, 0)
        between(n)

    for n in (3, 2, 1, 0):
        m = 3 - n

        def taps(zone, carry):
            for v in range(V):
                put_ring(ring.at[zone, v], sk[zone, 0] * sl[m, zone, v, 0])
            return carry

        lax.fori_loop(0, 2, taps, 0)

        def back(zone, carry):
            other = 1 - zone
            acc = [jnp.zeros((32, 128), F32)] * V
            t = shift[other, n]
            for j in range(6):
                put_ring(tring, tap[other, n, j])
                amount = (8192 - t - j) % 4096
                cj = shifted(tring, amount)
                for v in range(V):
                    acc[v] = acc[v] + cj * shifted(ring.at[other, v], amount)
            for v in range(V):
                face[zone, 15 + n * V + v] = acc[v]
            for k in range(n):
                cur = [sl[m, zone, v, k] for v in range(V)]
                kk = sk[zone, k]
                for v in range(V):
                    s = kk * cur[v]
                    lap = rows_beside(s) + sk[zone, k + 1] * sl[m, zone, v, k + 1] - 4.0 * s
                    if k == 0:
                        lap = lap + acc[v]
                    else:
                        lap = lap + sk[zone, k - 1] * sl[m, zone, v, k - 1]
                    if n == 3:
                        th = jnp.tanh(su[3, zone, v, k])
                        d = 1.0 - th * th
                    else:
                        d = sd[n, zone, v, k]
                    pulled = coup[0, v] * cur[0]
                    for w in range(1, V):
                        pulled = pulled + coup[w, v] * cur[w]
                    sl[m + 1, zone, v, k] = cur[v] + lap - d * pulled
            return carry

        if n > 0:
            lax.fori_loop(0, 2, back, 0)
        else:
            back(q, 0)


def face_columns(face, q, b, cols):
    pad = jnp.zeros((128 - 35, 128), F32)
    for part, dst, size, lo in (((b + 31) % 32, 8, 8, 120), (b, 16, 128, 0), ((b + 1) % 32, 144, 8, 0)):
        rows = face[q, pl.ds(part, 35, stride=32), :]
        cols[dst : dst + size, :] = jnp.concatenate([rows, pad], axis=0).T[lo : lo + size, :]


def scatter_points(hsum, l1, u0, area, proj, ids, dist, partial):
    lane = lane_of((128, 128))
    hs = [hsum[v, 16:144, :] + l1[v, 0, 16:144, :] * u0[v, 0, 16:144, :] for v in range(V)]
    acc = jnp.zeros((128, 128), F32)
    for c in range(3):
        col = proj[c, 0] * hs[0]
        for v in range(1, V):
            col = col + proj[c, v] * hs[v]
        acc = acc + jnp.where(lane == c, pltpu.roll(col, c, 1), 0.0)
    spread = (
        lax.broadcasted_iota(jnp.int32, (128, 384), 1) // 3 == lax.broadcasted_iota(jnp.int32, (128, 384), 0)
    ).astype(F32)
    sens = lax.dot_general(
        acc, spread, (((0,), (0,)), ((), ())), precision=lax.Precision.HIGHEST, preferred_element_type=F32
    )
    sens = [sens[c : c + 1, :] * area[...] for c in range(3)]
    sub_a = lax.broadcasted_iota(jnp.int32, (128, 128), 0)
    sub_b = lax.broadcasted_iota(jnp.int32, (256, 128), 0)
    total = jnp.zeros((384, 256), F32)
    for k in range(8):
        dk = dist[k : k + 1, :]
        om = 1.0 - dk
        om = om * om
        phi = om * om * (4.0 * dk + 1.0)
        idk = ids[k : k + 1, :]
        for wt in range(3):
            cut = slice(wt * 128, (wt + 1) * 128)
            idt = idk[:, cut]
            ch = idt // 256
            rowid = (ch % 2) * 64 + ((ch // 8) % 4) * 16 + ((ch // 2) % 4) * 4 + ch // 32
            mask = sub_a == rowid
            high, low = [], []
            for c in range(3):
                val = phi[:, cut] * sens[c][:, cut]
                hi = val.astype(jnp.bfloat16).astype(F32)
                high.append(jnp.where(mask, hi, 0.0).astype(jnp.bfloat16))
                low.append(jnp.where(mask, val - hi, 0.0).astype(jnp.bfloat16))
            left = jnp.concatenate([jnp.concatenate(high, axis=0), jnp.concatenate(low, axis=0)], axis=1)
            onehot = jnp.where(sub_b == idt % 256, 1.0, 0.0).astype(jnp.bfloat16)
            right = jnp.concatenate([onehot, onehot], axis=1)
            total = total + lax.dot_general(
                left, right, (((1,), (1,)), ((), ())), preferred_element_type=F32
            )
    for c in range(3):
        partial[c] = total[c * 128 : (c + 1) * 128, :]


def window_kernel(
    coup, proj, u_hbm, k_hbm, l_hbm, m_hbm, w_hbm, area, ids, dist, out_hbm, points,
    u0, u1, u2, u3, d0, d1, d2, l4, l3, l2, l1, s4, s3, s2, s1, kap, kc, hsum, outv,
    su, sd, sl, sk, tap, ring, tring, face, cols, shift,
    gat, hu, hl, hk, chunk, mt, wt, partial, r1, q1, r2, q2, r3, q3, r4, turned,
    sem, osem, halo_s, halo_r, first_s, first_r, ph_s, ph_r, core_s, core_r, rs_s, rs_r,
):
    y, b, x, z, c = place()
    q = y % 2
    yp = y + 1 - 2 * q
    b0 = b - c
    twin = b0 + 1 - c
    nxt, prv = (b + 1) % 32, (b + 31) % 32
    us, ds, ls, ss = (u0, u1, u2, u3), (d0, d1, d2), (l4, l3, l2, l1), (s4, s3, s2, s1)

    def loads_of(t):
        cut = pl.ds(t * 128, 128)
        own = pl.ds(16, 128)
        return [
            pltpu.make_async_copy(u_hbm.at[:, 0, :, cut], u0.at[:, t, own, :], sem.at[3 * t]),
            pltpu.make_async_copy(l_hbm.at[:, 0, :, cut], l4.at[:, t, own, :], sem.at[3 * t + 1]),
            pltpu.make_async_copy(k_hbm.at[0, :, cut], kap.at[t, own, :], sem.at[3 * t + 2]),
        ]

    mine = pl.ds(pl.multiple_of(b * 128, 128), 128)
    maps = [
        pltpu.make_async_copy(m_hbm.at[:, 0, mine], mt, sem.at[12]),
        pltpu.make_async_copy(w_hbm.at[:, 0, mine], wt, sem.at[13]),
    ]
    loads = [loads_of(t) for t in range(4)]
    for copy in loads[3] + maps + loads[0] + loads[1] + loads[2]:
        copy.start()

    barrier = pltpu.get_barrier_semaphore()
    peers = [(y, nxt), (y, prv), (yp, b0), (yp, b0 + 1), (y, twin)]
    for d in (1, 2, 3):
        peers.append((y, block_of((x + d) % 4, z, c)))
        peers.append((y, block_of(x, (z + d) % 4, c)))
        peers.append(((y + d) % 4, b))
    for peer in peers:
        pl.semaphore_signal(barrier, inc=1, device_id=peer, device_id_type=MESH)

    halo = []
    for n, (src, dst) in enumerate(((u_hbm, hu), (l_hbm, hl), (k_hbm, hk))):

        def rows(r):
            return src.at[:, 0, pl.ds(r, 8), :] if len(src.shape) == 4 else src.at[0, pl.ds(r, 8), :]

        halo.append(remote(rows(120), dst.at[0], halo_s.at[n], halo_r.at[n], y, nxt))
        halo.append(remote(rows(0), dst.at[1], halo_s.at[3 + n], halo_r.at[3 + n], y, prv))

    for copy in loads[3] + maps:
        copy.wait()
    for v in range(V):
        chunk[KU * v : KU * (v + 1), :] = u0[v, 3, 16:144, :].T[128 - KU :, :]
        chunk[OFF_L + KL * v : OFF_L + KL * (v + 1), :] = l4[v, 3, 16:144, :].T[128 - KL :, :]
    chunk[OFF_K : OFF_K + KU, :] = kap[3, 16:144, :].T[128 - KU :, :]
    chunk[OFF_M : OFF_M + 4, :] = mt[...].astype(F32)
    chunk[OFF_W : OFF_W + 4, :] = wt[...]

    for copy in loads[0] + loads[1] + loads[2]:
        copy.wait()

    def scale(i):
        rows = pl.ds(pl.multiple_of(8 + i * 8, 8), 8)
        for t in range(4):
            k = kap[t, rows, :]
            kc[t, rows, :] = 1.0 - 4.0 * k
            for v in range(V):
                s4[v, t, rows, :] = k * l4[v, t, rows, :]

    every = (0, 1, 2, 3)
    over_rows(scale, 1, 16, 2)
    main_forward(0, us, ds, kap, kc, coup, every, None, inner(2))
    pl.semaphore_wait(barrier, len(peers))

    here = gat.at[q, x, z * 2 + c]
    across = remote(chunk, here, first_s.at[0], first_r.at[c], yp, b0 + q)
    across.start()
    for copy in halo:
        copy.start()

    @pl.when(c == q)
    def _():
        gat[q, x, z * 2 + c] = chunk[...]

    @pl.when(c != q)
    def _():
        remote(chunk, here, first_s.at[1], first_r.at[2], y, b0 + q).start()

    def part(core, stage, d):
        if core == 0:
            if stage == 0:
                return gat.at[0, (x + d) % 4, pl.ds(z * 2, 2)]
            return gat.at[0, :, pl.ds((z + d) % 4 * 2, 2)]
        if stage == 0:
            return gat.at[1, x, pl.ds((z + d) % 4 * 2, 2)]
        return gat.at[1, (x + d) % 4]

    def hops(core, stage):
        copies = []
        for d in (1, 2, 3):
            to = block_of((x + d) % 4, z, c) if core == stage else block_of(x, (z + d) % 4, c)
            n = 3 * stage + d - 1
            copies.append(remote(part(core, stage, 0), part(core, stage, 0), ph_s.at[n], ph_r.at[n], y, to))
        return copies

    def swaps(core, whose):
        return [
            remote(part(whose, 1, d), part(whose, 1, d), core_s.at[d], core_r.at[d], y, twin) for d in range(4)
        ]

    def on_core(core, action):
        @pl.when(c == core)
        def _():
            action(core)

    def first_stage(core):
        @pl.when(q == core)
        def _():
            remote(chunk, here, first_s.at[1], first_r.at[2], y, b0 + q).wait_recv()

        @pl.when(q != core)
        def _():
            for j in range(2):
                remote(chunk, here, first_s.at[0], first_r.at[j], yp, b0 + q).wait_recv()

        for copy in hops(core, 0):
            copy.start()

    def second_stage(core):
        for copy in hops(core, 0):
            copy.wait()
        for copy in hops(core, 1):
            copy.start()
        swaps(core, core)[0].start()

    def third_stage(core):
        copies, sends = hops(core, 1), swaps(core, core)
        for copy in copies:
            copy.wait()
        for copy in sends[1:]:
            copy.start()

    def last_stage(core):
        for copy in swaps(core, core):
            copy.wait_send()
        for copy in swaps(core, 1 - core):
            copy.wait_recv()

    main_forward(1, us, ds, kap, kc, coup, every, None, inner(3))
    for core in range(2):
        on_core(core, first_stage)
    main_forward(2, us, ds, kap, kc, coup, every, None, inner(4))

    for n in (3, 2, 1):
        main_adjoint(n, us, ds, ls, ss, kap, kc, coup, every, None, None, outv, inner(8 - n))

    for core in range(2):
        on_core(core, second_stage)

    for copy in halo:
        copy.wait()
    for t in range(4):
        cut = slice(t * 128, (t + 1) * 128)
        for side, r in ((0, 8), (1, 144)):
            kap[t, r : r + 8, :] = hk[side, :, cut]
            for v in range(V):
                u0[v, t, r : r + 8, :] = hu[side, v, :, cut]
                l4[v, t, r : r + 8, :] = hl[side, v, :, cut]

    over_edges(scale, 1)
    for n in range(3):
        main_forward(n, us, ds, kap, kc, coup, every, None, edges(n + 2))

    for n in (3, 2, 1):
        main_adjoint(n, us, ds, ls, ss, kap, kc, coup, (0,), None, hsum, outv)
    scatter_points(hsum, l1, u0, area, proj, ids, dist, partial)
    first = remote(
        partial.at[:, pl.ds(pl.multiple_of((1 - c) * 64, 64), 64), :], r1, rs_s.at[0], rs_r.at[0], y, twin
    )
    first.start()

    def sent(slots, got, base, to_of):
        copies = []
        for d in (1, 2, 3):
            index, ty, tb = to_of(d)
            copies.append(
                remote(slots.at[index], got.at[d - 1], rs_s.at[base + d], rs_r.at[base + d], ty, tb)
            )
        return copies

    by_x = sent(q1, r2, 0, lambda d: ((x + d) % 4, y, block_of((x + d) % 4, z, c)))
    by_z = sent(q2, r3, 3, lambda d: ((z + d) % 4, y, block_of(x, (z + d) % 4, c)))
    by_y = sent(q3, r4, 6, lambda d: ((y + d) % 4, (y + d) % 4, b))

    def reduce_stage(step):
        if step == 0:
            first.wait()
            own = pl.multiple_of(c * 64, 64)
            for j in range(4):
                q1[j] = partial[:, pl.ds(own + j * 16, 16), :] + r1[:, j * 16 : (j + 1) * 16, :]
            for copy in by_x:
                copy.start()
        if step == 1:
            for copy in by_x:
                copy.wait()
            total = q1[x] + r2[0] + r2[1] + r2[2]
            for j in range(4):
                q2[j] = total[:, j * 4 : (j + 1) * 4, :]
            for copy in by_z:
                copy.start()
        if step == 2:
            for copy in by_z:
                copy.wait()
            total = q2[z] + r3[0] + r3[1] + r3[2]
            for j in range(4):
                q3[j] = total[:, j, :]
            for copy in by_y:
                copy.start()
        if step == 3:
            for copy in by_y:
                copy.wait()
            points[...] = q3[y] + r4[0] + r4[1] + r4[2]

    for n in (3, 2, 1, 0):
        rest = None if n == 0 else edges(8 - n)
        main_adjoint(n, us, ds, ls, ss, kap, kc, coup, every, None, None, outv, rest)
        if n == 2:
            reduce_stage(0)
            for core in range(2):
                on_core(core, third_stage)
    for core in range(2):
        on_core(core, last_stage)
    across.wait_send()

    @pl.when(c != q)
    def _():
        remote(chunk, here, first_s.at[1], first_r.at[2], y, b0 + q).wait_send()


    def between(n):
        if n == 0:
            reduce_stage(1)
        if n == 2:
            reduce_stage(2)

    strips(gat, q, coup, su, sd, sl, sk, tap, shift, ring, tring, face, turned, between)
    face_columns(face.reshape(2, 35 * 32, 128), q, b, cols)
    stores = [
        pltpu.make_async_copy(outv.at[:, t], out_hbm.at[:, 0, :, pl.ds(t * 128, 128)], osem.at[t])
        for t in range(4)
    ]
    for copy in stores[:3]:
        copy.start()
    for n in range(3):
        main_forward(n, us, ds, kap, kc, coup, (3,), cols, all_rows)
    for n in (3, 2, 1, 0):
        main_adjoint(n, us, ds, ls, ss, kap, kc, coup, (3,), cols, None, outv)
    stores[3].start()
    reduce_stage(3)
    for copy in stores:
        copy.wait()


def local(
    start_state, diffusivity, donor_map, donor_weight, coupling, final_cotangent,
    wall_area, wall_projection, center_ids, center_dist,
):
    any_ = pl.BlockSpec(memory_space=pl.ANY)
    vmem = pl.BlockSpec(memory_space=pltpu.VMEM)
    smem = pl.BlockSpec(memory_space=pltpu.SMEM)
    dma = pltpu.SemaphoreType.DMA

    def buf(*shape, dtype=F32):
        return pltpu.VMEM(shape, dtype)

    return pl.pallas_call(
        window_kernel,
        out_shape=(jax.ShapeDtypeStruct((V, 1, 128, 512), F32), jax.ShapeDtypeStruct((3, 256), F32)),
        in_specs=[smem, smem, any_, any_, any_, any_, any_, vmem, vmem, vmem],
        out_specs=(any_, vmem),
        scratch_shapes=[buf(V, 4, ROWS, 128)] * 15
        + [
            buf(4, ROWS, 128),
            buf(4, ROWS, 128),
            buf(V, ROWS, 128),
            buf(V, 4, 128, 128),
            buf(4, 2, V, KU, 32, 128),
            buf(3, 2, V, 2, 32, 128),
            buf(4, 2, V, KL, 32, 128),
            buf(2, KU, 32, 128),
            buf(2, 4, 6, 32, 128),
            buf(2, V, 72, 128),
            buf(72, 128),
            buf(2, 35, 32, 128),
            buf(ROWS, 128),
            pltpu.SMEM((2, 4), jnp.int32),
            buf(2, 4, 8, CHUNK, 128),
            buf(2, V, 8, 512),
            buf(2, V, 8, 512),
            buf(2, 8, 512),
            buf(CHUNK, 128),
            buf(4, 128, dtype=jnp.int32),
            buf(4, 128),
            buf(3, 128, 256),
            buf(3, 64, 256),
            buf(4, 3, 16, 256),
            buf(3, 3, 16, 256),
            buf(4, 3, 4, 256),
            buf(3, 3, 4, 256),
            buf(4, 3, 256),
            buf(3, 3, 256),
            buf(CHUNK, 32, 128),
        ]
        + [dma((n,)) for n in (14, 4, 6, 6, 2, 3, 6, 6, 4, 4, 10, 10)],
        compiler_params=pltpu.CompilerParams(
            collective_id=0, has_side_effects=True, vmem_limit_bytes=60 * 1024 * 1024
        ),
        name="window",
    )(
        coupling, wall_projection, start_state, diffusivity, final_cotangent, donor_map, donor_weight,
        wall_area, center_ids[0], center_dist[0],
    )


def solution(mesh):
    return jax.shard_map(
        local,
        mesh=mesh,
        in_specs=(
            P(None, "zone", "block", None),
            P("zone", "block", None),
            P(None, "zone", None),
            P(None, "zone", None),
            P(),
            P(None, "zone", "block", None),
            P("zone", "block"),
            P(),
            P("zone", None, "block"),
            P("zone", None, "block"),
        ),
        out_specs=(P(None, "zone", "block", None), P(None, ("zone", "block"))),
        check_vma=False,
    )
```
